128 devices in a mesh: seq: 8 (over y, core), vocab: 16 (over x, z).
Axes of the slice: x: 4, y: 4, z: 4, core: 2. Of those that a mesh axis runs over, the one named last changes fastest.
Arguments:
- queries: bfloat16 [8192, 2, 2048], P(('seq', 'vocab')), may hold values from -40 to 40
- key_vectors: bfloat16 [8192, 2, 2048], P(('seq', 'vocab')), may hold values from -40 to 40
- value_vectors: bfloat16 [8192, 2, 2048], P(('seq', 'vocab')), may hold values from -18 to 18
- residual: bfloat16 [8192, 2, 2048], P(('seq', 'vocab')), may hold values from -3 to 3
- norm_gain: float32 [2048], replicated, may hold values from 0.1 to 1.9
- head_weight: bfloat16 [2048, 16384], P(None, 'vocab'), may hold values from -0.125 to 0.125
- head_bias: float32 [16384], P('vocab'), may hold values from -6 to 6
- doc_lengths: int32 [2], replicated, may hold values from 1 to 8192, 12288 in all
Outputs:
- pooled: float32 [2, 16384], P(None, 'vocab')
- grad_hidden: bfloat16 [8192, 2, 2048], P(('seq', 'vocab'))
The draws below stay inside these ranges and needn't reach their ends.
Inputs may be any that keep to these rules, and one draw needn't show every extreme that they name: `doc_lengths`: the lengths add up to 12288.
All inputs are finite; a program needn't handle non-finite values.
Results may differ from the reference program's by a relative error of at most 0.018.
Values may be sent and summed in bfloat16 or wider, within the bound.
No kernel may reach another device: no remote copies, remote signals or barrier semaphores. Data moves between devices by JAX's collectives and lax.ppermute only.
A program may use at most 128 MiB of HBM per device.

```python
import math
import jax
import jax.numpy as jnp
import numpy as np
from jax import lax

D = 2048
HEADS = 16
HEAD_DIM = 128
DOCS = 2
LENGTH = 8192
VOCAB = 16384


def draw_pair(key):
    key_query, key_key = jax.random.split(jax.random.fold_in(key, 7), 2)
    shape = (LENGTH, DOCS, D)
    query_draw = 1.3 * jax.random.normal(key_query, shape, jnp.float32)
    key_draw = 1.3 * jax.random.normal(key_key, shape, jnp.float32)
    return (jnp.clip(query_draw, -40.0, 40.0), jnp.clip(key_draw, -40.0, 40.0))


def draw_queries(key, part):
    return draw_pair(key)[0].astype(jnp.bfloat16)


def draw_key_vectors(key, part):
    return draw_pair(key)[1].astype(jnp.bfloat16)


def level_of(own_key, dims, cuts, least, largest):
    gain = 1.0
    for position, shards_of in cuts:
        draws = jax.random.uniform(jax.random.fold_in(jax.random.fold_in(own_key, 6), position), (shards_of,), jnp.float32, least / len(cuts), largest / len(cuts))
        gain = gain * jnp.repeat(jnp.exp(draws), dims[position] // shards_of).reshape((-1,) + (1,) * (len(dims) - 1 - position))
    return gain


def split_up(amount, total, reach, skew):
    weights = [(1 << 20) // math.isqrt(rank ** skew) + 1 for rank in range(2, amount + 1)]
    spare, holding = total - reach - (amount - 1), [1] * (amount - 1)
    while spare > 0:
        free = [i for i in range(amount - 1) if holding[i] < reach]
        whole, budget = sum([weights[i] for i in free]), spare
        for i in free:
            more = min(reach - holding[i], max(1, budget * weights[i] // whole), spare)
            holding[i] = holding[i] + more
            spare = spare - more
    return np.array([reach] + holding)


def ragged_sizes(stream_key, number_of, total, limit, skew):
    if number_of == 2:
        one = jax.random.randint(stream_key, (), max(1, total - limit), min(limit, total - 1) + 1)
        return jnp.stack([one, total - one])
    sizes = jnp.asarray(split_up(number_of, total, limit, skew), jnp.int32)
    twos = (number_of - 1) // 2
    giver, receiver = sizes[1:1 + 2 * twos:2], sizes[2:2 + 2 * twos:2]
    room = jnp.minimum(giver - 1, limit - receiver)
    moved = jax.random.randint(jax.random.fold_in(stream_key, 1), (twos,), 0, 1 << 20) % (room + 1)
    sizes = sizes.at[1:1 + 2 * twos:2].set(giver - moved).at[2:2 + 2 * twos:2].set(receiver + moved)
    return sizes[jax.random.permutation(jax.random.fold_in(stream_key, 2), number_of)]


def scatter_about(rng, dims, scale, limit, cuts=(), held_as=jnp.bfloat16):
    drawn = jax.random.normal(rng, dims, jnp.float32) * scale
    if len(cuts) > 0:
        drawn = level_of(rng, dims, cuts, -0.22, 0.18) * drawn
    return jnp.clip(drawn, min=-limit, max=limit).astype(held_as)


def setup_inputs(seed: int = 0) -> dict:
    seeds = jax.random.split(jax.random.key(seed), 9)
    queries = draw_queries(jax.random.fold_in(seeds[8], 71), 0)
    key_vectors = draw_key_vectors(jax.random.fold_in(seeds[8], 71), 0)
    value_vectors = scatter_about(seeds[2], (LENGTH, DOCS, D), 3.0, 18.0, ((0, 128),))
    residual = scatter_about(seeds[3], (LENGTH, DOCS, D), 0.5, 3.0, ((0, 128),))
    norm_gain = jnp.clip(1.0 + 0.18 * jax.random.normal(seeds[4], (D,), jnp.float32), 0.1, 1.9)
    head_weight = scatter_about(seeds[5], (D, VOCAB), D ** -0.5, 0.125, ((1, 16),))
    head_bias = scatter_about(seeds[6], (VOCAB,), 1.0, 6.0, ((0, 16),), jnp.float32)
    doc_lengths = ragged_sizes(seeds[7], DOCS, 3 * DOCS * LENGTH // 4, LENGTH, 0).astype(jnp.int32)
    return dict(queries=queries, key_vectors=key_vectors, value_vectors=value_vectors, residual=residual, norm_gain=norm_gain, head_weight=head_weight, head_bias=head_bias, doc_lengths=doc_lengths)


sharpness = 8.0
flops_weight = 500.0
epsilon = 1e-05

def attend_doc(inputs):
    query_head, key_head, value_head, key_allowed = inputs
    scores = jnp.dot(query_head, key_head.T) / math.sqrt(HEAD_DIM)
    allowed = key_allowed[None, :]
    highest = lax.optimization_barrier(jnp.max(jnp.where(allowed, scores, -1e+30), axis=1, keepdims=True))
    weights = jnp.where(allowed, jnp.exp(scores - highest), 0.0)
    weight_sum = lax.optimization_barrier(jnp.sum(weights, axis=1))
    rounded = weights.astype(jnp.bfloat16).astype(jnp.float32)
    summed = jnp.dot(rounded, value_head)
    return (summed / weight_sum[:, None]).astype(jnp.bfloat16)

def attention_head(queries, key_vectors, value_vectors, key_allowed, head_index):
    offset = (head_index * HEAD_DIM).astype(jnp.int32)
    query_head = jnp.transpose(lax.dynamic_slice_in_dim(queries, offset, HEAD_DIM, 2), (1, 0, 2)).astype(jnp.float32)
    key_head = jnp.transpose(lax.dynamic_slice_in_dim(key_vectors, offset, HEAD_DIM, 2), (1, 0, 2)).astype(jnp.float32)
    value_head = jnp.transpose(lax.dynamic_slice_in_dim(value_vectors, offset, HEAD_DIM, 2), (1, 0, 2)).astype(jnp.float32)
    return lax.map(attend_doc, (query_head, key_head, value_head, key_allowed))

def reference(queries, key_vectors, value_vectors, residual, norm_gain, head_weight, head_bias, doc_lengths):
    slot_index = jnp.arange(LENGTH, dtype=jnp.int32)
    key_allowed = slot_index[None, :] < doc_lengths[:, None]
    per_head = lax.map(lambda head_index: attention_head(queries, key_vectors, value_vectors, key_allowed, head_index), jnp.arange(HEADS, dtype=jnp.int32))
    attended = jnp.transpose(per_head, (2, 1, 0, 3)).reshape(LENGTH, DOCS, D)
    combined = residual.astype(jnp.float32) + attended.astype(jnp.float32)
    inv_rms = lax.rsqrt(lax.optimization_barrier(jnp.mean(combined * combined, axis=2, keepdims=True)) + epsilon)
    hidden = (combined * inv_rms * norm_gain).astype(jnp.bfloat16)
    hidden_docs = jnp.transpose(hidden, (1, 0, 2))

    def boosted_of(hidden_doc, length_doc):
        logits = jnp.dot(hidden_doc, head_weight, preferred_element_type=jnp.float32) + head_bias
        saturated = jnp.log1p(jnp.maximum(logits, 0.0))
        row_allowed = slot_index[:, None] < length_doc
        boosted = jnp.where(row_allowed, jnp.exp(sharpness * saturated), 0.0)
        return (logits, boosted)

    def total_of(inputs):
        hidden_doc, length_doc = inputs
        return lax.optimization_barrier(jnp.sum(boosted_of(hidden_doc, length_doc)[1], axis=0))
    totals = lax.map(total_of, (hidden_docs, doc_lengths))
    pooled = jnp.log(totals / doc_lengths[:, None].astype(jnp.float32)) / sharpness
    usage = lax.optimization_barrier(jnp.mean(pooled, axis=0))
    coefficient = 2.0 * flops_weight / DOCS * usage[None, :] / totals

    def gradient_of(inputs):
        hidden_doc, length_doc, coefficient_doc = inputs
        logits, boosted = boosted_of(hidden_doc, length_doc)
        derivative = jnp.where(logits > 0.0, 1.0 / (1.0 + jnp.maximum(logits, 0.0)), 0.0)
        dlogits = (coefficient_doc[None, :] * boosted * derivative).astype(jnp.bfloat16)
        grad_rows = lax.dot_general(dlogits, head_weight, (((1,), (1,)), ((), ())), preferred_element_type=jnp.float32)
        return grad_rows.astype(jnp.bfloat16)
    grad_docs = lax.map(gradient_of, (hidden_docs, doc_lengths, coefficient))
    grad_hidden = jnp.transpose(grad_docs, (1, 0, 2))
    return (pooled, grad_hidden)
```

```python
import math

import jax
import jax.numpy as jnp
from jax import lax
from jax.experimental import pallas as pl
from jax.experimental.pallas import tpu as pltpu
from jax.sharding import Mesh
from jax.sharding import PartitionSpec as P

HEAD_DIM = 128
AXES = ("y", "c", "x", "z")
PLANE = ("c", "x", "z")
LOW = -1e30

sharpness = 8.0
flops_weight = 500.0
epsilon = 1e-05


def shift_perm(sizes, **by):
    steps = [by.get(axis, 0) for axis in AXES]
    pairs = []
    for source in range(math.prod(sizes)):
        rest, place = source, []
        for size in reversed(sizes):
            place.append(rest % size)
            rest //= size
        target = 0
        for size, at, step in zip(sizes, reversed(place), steps):
            target = target * size + (at + step) % size
        pairs.append((source, target))
    return pairs


def attention_kernel(first, last, chunks, sub, counts, q_ref, *refs):
    keys = refs[: 2 * chunks : 2]
    values = refs[1 : 2 * chunks : 2]
    rest = list(refs[2 * chunks :])
    if not first:
        top_in, sum_in = rest.pop(0), rest.pop(0)
    if last:
        out_ref = rest.pop(0)
        top_ref, sum_ref = rest.pop(0), rest.pop(0)
    else:
        top_ref, sum_ref = rest.pop(0), rest.pop(0)
    wide = rest.pop(0)
    step = pl.program_id(0)
    rows = top_ref.shape[0]
    depth = wide.shape[1]
    scale = math.log2(math.e) / math.sqrt(HEAD_DIM)

    @pl.when(step == 0)
    def _():
        for n in range(chunks):
            wide[n, :, :HEAD_DIM] = values[n][...].reshape(depth, HEAD_DIM)
            wide[n, :, HEAD_DIM:] = jnp.ones((depth, HEAD_DIM), wide.dtype)

    if first:
        top_ref[...] = jnp.full_like(top_ref, LOW)
        sum_ref[...] = jnp.zeros_like(sum_ref)
    else:
        top_ref[...] = top_in[...]
        sum_ref[...] = sum_in[...]
    queries_real = counts[0] > step * rows

    def attend(n, masked):
        key = keys[n][...].reshape(depth, HEAD_DIM)
        for at in range(0, rows, sub):
            query = q_ref[at // 64 : (at + sub) // 64].reshape(sub, HEAD_DIM)
            scores = lax.dot_general(
                query, key, (((1,), (1,)), ((), ())), preferred_element_type=jnp.float32
            )
            if masked:
                place = lax.broadcasted_iota(jnp.int32, scores.shape, 1)
                scores = jnp.where(place < counts[1 + n], scores, LOW)
            old_top = top_ref[pl.ds(at, sub), :]
            new_top = jnp.maximum(old_top, jnp.max(scores, axis=1, keepdims=True))
            weights = jnp.exp2((scores - new_top[:, :1]) * scale)
            shrink = jnp.exp2((old_top - new_top) * scale)
            added = jnp.dot(
                weights.astype(jnp.bfloat16), wide[n], preferred_element_type=jnp.float32
            )
            top_ref[pl.ds(at, sub), :] = new_top
            for part in range(0, 2 * HEAD_DIM, HEAD_DIM):
                cols = pl.ds(part, HEAD_DIM)
                sum_ref[pl.ds(at, sub), cols] = (
                    sum_ref[pl.ds(at, sub), cols] * shrink + added[:, part : part + HEAD_DIM]
                )

    for n in range(chunks):

        @pl.when(jnp.logical_and(queries_real, counts[1 + n] >= depth))
        def _():
            attend(n, False)

        @pl.when(
            jnp.logical_and(
                queries_real, jnp.logical_and(counts[1 + n] > 0, counts[1 + n] < depth)
            )
        )
        def _():
            attend(n, True)

    if last:

        @pl.when(queries_real)
        def _():
            done = sum_ref[:, :HEAD_DIM] / sum_ref[:, HEAD_DIM:]
            out_ref[...] = done.astype(out_ref.dtype).reshape(out_ref.shape)

        @pl.when(jnp.logical_not(queries_real))
        def _():
            out_ref[...] = jnp.zeros_like(out_ref)


def attend_chunks(counts, qkv, pairs, carry, last, block=512, sub=256):
    sources, parts, tokens = qkv.shape[0], qkv.shape[1], qkv.shape[2]
    total = sources * tokens
    first = carry is None
    chunks = len(pairs) // 2

    def whole(array, part):
        if array.ndim == 4:
            return pl.BlockSpec(
                (sources, None, tokens, HEAD_DIM), lambda i, counts: (0, part, 0, 0)
            )
        return pl.BlockSpec((sources, tokens, HEAD_DIM), lambda i, counts: (0, 0, 0))

    in_specs = [
        pl.BlockSpec((block // tokens, None, tokens, HEAD_DIM), lambda i, counts: (i, 0, 0, 0))
    ]
    operands = [qkv]
    for array, part in pairs:
        in_specs.append(whole(array, part))
        operands.append(array)
    top_spec = pl.BlockSpec((block, HEAD_DIM), lambda i, counts: (i, 0))
    sum_spec = pl.BlockSpec((block, 2 * HEAD_DIM), lambda i, counts: (i, 0))
    if not first:
        in_specs += [top_spec, sum_spec]
        operands += list(carry)
    scratch = [pltpu.VMEM((chunks, total, 2 * HEAD_DIM), jnp.bfloat16)]
    if last:
        out_specs = pl.BlockSpec((block // tokens, tokens, HEAD_DIM), lambda i, counts: (i, 0, 0))
        out_shape = jax.ShapeDtypeStruct((sources, tokens, HEAD_DIM), jnp.bfloat16)
        scratch = [
            pltpu.VMEM((block, HEAD_DIM), jnp.float32),
            pltpu.VMEM((block, 2 * HEAD_DIM), jnp.float32),
        ] + scratch
    else:
        out_specs = [top_spec, sum_spec]
        out_shape = [
            jax.ShapeDtypeStruct((total, HEAD_DIM), jnp.float32),
            jax.ShapeDtypeStruct((total, 2 * HEAD_DIM), jnp.float32),
        ]

    def body(*refs):
        attention_kernel(first, last, chunks, sub, *refs)

    return pl.pallas_call(
        body,
        grid_spec=pltpu.PrefetchScalarGridSpec(
            num_scalar_prefetch=1,
            grid=(total // block,),
            in_specs=in_specs,
            out_specs=out_specs,
            scratch_shapes=scratch,
        ),
        out_shape=out_shape,
        cost_estimate=pl.CostEstimate(
            flops=8 * total * total * HEAD_DIM * chunks,
            bytes_accessed=4 << 20,
            transcendentals=total * total * chunks,
        ),
        compiler_params=pltpu.CompilerParams(vmem_limit_bytes=48 << 20),
        name="attend_last" if last else ("attend_first" if first else "attend_next"),
    )(counts, *operands)


def local(
    queries, key_vectors, value_vectors, residual, norm_gain, head_weight, head_bias, doc_lengths
):
    tokens, docs, width = queries.shape
    heads = width // HEAD_DIM
    sizes = [lax.axis_size(axis) for axis in AXES]
    y_size, c_size, x_size, z_size = sizes
    plane = c_size * x_size * z_size
    y_at, c_at, x_at, z_at = [lax.axis_index(axis) for axis in AXES]

    def by_head(array):
        return jnp.transpose(array.reshape(tokens, docs, heads, HEAD_DIM), (1, 2, 0, 3)).reshape(
            docs * heads, tokens, HEAD_DIM
        )

    def move(array, **by):
        return lax.ppermute(array, AXES, shift_perm(sizes, **by))

    stacked = jnp.stack([by_head(a) for a in (queries, key_vectors, value_vectors)], axis=1)
    qkv = lax.all_to_all(stacked, PLANE, split_axis=0, concat_axis=0, tiled=True)
    block_rows = plane * tokens
    length = doc_lengths[c_at]

    def real(quarter):
        return jnp.clip(length - (quarter % y_size) * block_rows, 0, block_rows)

    mine = real(y_at)
    key_own, value_own = qkv[:, 1], qkv[:, 2]
    key_left = move(key_own, y=1)
    value_right = move(value_own, y=-1)
    value_left = move(value_own, y=1)
    key_right = move(key_own, y=-1)
    key_far = move(key_left, y=1)
    value_far = move(value_right, y=-1)
    carry = attend_chunks(jnp.stack([mine, mine]), qkv, [(qkv, 1), (qkv, 2)], None, False)
    carry = attend_chunks(
        jnp.stack([mine, real(y_at - 1), real(y_at + 1)]),
        qkv,
        [(key_left, 0), (value_left, 0), (key_right, 0), (value_right, 0)],
        carry,
        False,
    )
    attended = attend_chunks(
        jnp.stack([mine, real(y_at + 2)]), qkv, [(key_far, 0), (value_far, 0)], carry, True
    )
    back = lax.all_to_all(attended, PLANE, split_axis=0, concat_axis=0, tiled=True)
    returned = jnp.transpose(back.reshape(docs, heads, tokens, HEAD_DIM), (2, 0, 1, 3)).reshape(
        tokens, docs, width
    )
    combined = residual.astype(jnp.float32) + returned.astype(jnp.float32)
    inv_rms = lax.rsqrt(jnp.mean(combined * combined, axis=2, keepdims=True) + epsilon)
    hidden = (combined * inv_rms * norm_gain).astype(jnp.bfloat16)
    arrived = lax.all_gather(hidden, ("x", "z"), axis=0, tiled=True)
    row_count = arrived.shape[0]
    flattened = jnp.dot(
        arrived.reshape(row_count * docs, width), head_weight, preferred_element_type=jnp.float32
    )
    logits = flattened.reshape(row_count, docs, head_weight.shape[1]) + head_bias
    row_index = jnp.arange(row_count, dtype=jnp.int32)
    position = (y_at * c_size + c_at) * row_count + row_index
    row_allowed = position[:, None] < doc_lengths[None, :]
    saturated = jnp.log1p(jnp.maximum(logits, 0.0))
    boosted = jnp.where(row_allowed[:, :, None], jnp.exp(sharpness * saturated), 0.0)
    partial_sums = jnp.sum(boosted, axis=0)
    lengths_float = doc_lengths[:, None].astype(jnp.float32)
    totals = lax.psum(partial_sums, ("y", "c"))
    pooled = jnp.log(totals / lengths_float) / sharpness
    coefficient = 2.0 * flops_weight / docs * jnp.mean(pooled, axis=0)[None, :] / totals
    derivative = jnp.where(logits > 0.0, 1.0 / (1.0 + jnp.maximum(logits, 0.0)), 0.0)
    dlogits = (coefficient[None, :, :] * boosted * derivative).astype(jnp.bfloat16)
    flattened = lax.dot_general(
        dlogits.reshape(row_count * docs, dlogits.shape[2]),
        head_weight,
        (((1,), (1,)), ((), ())),
        preferred_element_type=jnp.float32,
    )
    own_rows = lax.psum_scatter(
        flattened.reshape(row_count, docs, width).astype(jnp.bfloat16),
        ("x", "z"),
        scatter_dimension=0,
        tiled=True,
    )
    return (pooled, own_rows)


def solution(mesh):
    grid = Mesh(mesh.devices.reshape(4, 2, 4, 4), AXES)
    rows = P(AXES, None, None)
    in_specs = (rows, rows, rows, rows, P(), P(None, ("x", "z")), P(("x", "z")), P())
    out_specs = (P(None, ("x", "z")), rows)
    return jax.shard_map(local, mesh=grid, in_specs=in_specs, out_specs=out_specs, check_vma=False)
```

```python
import math

import jax
import jax.numpy as jnp
from jax import lax
from jax.experimental import pallas as pl
from jax.experimental.pallas import tpu as pltpu
from jax.sharding import Mesh
from jax.sharding import PartitionSpec as P

HEAD_DIM = 128
AXES = ("y", "c", "u", "w", "z")
PLANE = ("c", "u", "w", "z")
LOW = -1e30

sharpness = 8.0
flops_weight = 500.0
epsilon = 1e-05


def shift_perm(sizes, **by):
    steps = [by.get(axis, 0) for axis in AXES]
    pairs = []
    for source in range(math.prod(sizes)):
        rest, place = source, []
        for size in reversed(sizes):
            place.append(rest % size)
            rest //= size
        target = 0
        for size, at, step in zip(sizes, reversed(place), steps):
            target = target * size + (at + step) % size
        pairs.append((source, target))
    return pairs


def attention_kernel(first, last, chunks, sub, counts, q_ref, *refs):
    keys = refs[: 2 * chunks : 2]
    values = refs[1 : 2 * chunks : 2]
    rest = list(refs[2 * chunks :])
    if not first:
        top_in, sum_in = rest.pop(0), rest.pop(0)
    if last:
        out_ref = rest.pop(0)
        top_ref, sum_ref = rest.pop(0), rest.pop(0)
    else:
        top_ref, sum_ref = rest.pop(0), rest.pop(0)
    wide = rest.pop(0)
    step = pl.program_id(0)
    rows = top_ref.shape[0]
    depth = wide.shape[1]
    scale = math.log2(math.e) / math.sqrt(HEAD_DIM)

    @pl.when(step == 0)
    def _():
        for n in range(chunks):
            wide[n, :, :HEAD_DIM] = values[n][...].reshape(depth, HEAD_DIM)
            wide[n, :, HEAD_DIM:] = jnp.ones((depth, HEAD_DIM), wide.dtype)

    if first:
        top_ref[...] = jnp.full_like(top_ref, LOW)
        sum_ref[...] = jnp.zeros_like(sum_ref)
    else:
        top_ref[...] = top_in[...]
        sum_ref[...] = sum_in[...]
    queries_real = counts[0] > step * rows

    def attend(n, masked):
        key = keys[n][...].reshape(depth, HEAD_DIM)
        for at in range(0, rows, sub):
            query = q_ref[at // 64 : (at + sub) // 64].reshape(sub, HEAD_DIM)
            scores = lax.dot_general(
                query, key, (((1,), (1,)), ((), ())), preferred_element_type=jnp.float32
            )
            if masked:
                place = lax.broadcasted_iota(jnp.int32, scores.shape, 1)
                scores = jnp.where(place < counts[1 + n], scores, LOW)
            old_top = top_ref[pl.ds(at, sub), :]
            new_top = jnp.maximum(old_top, jnp.max(scores, axis=1, keepdims=True))
            weights = jnp.exp2((scores - new_top[:, :1]) * scale)
            shrink = jnp.exp2((old_top - new_top) * scale)
            added = jnp.dot(
                weights.astype(jnp.bfloat16), wide[n], preferred_element_type=jnp.float32
            )
            top_ref[pl.ds(at, sub), :] = new_top
            for part in range(0, 2 * HEAD_DIM, HEAD_DIM):
                cols = pl.ds(part, HEAD_DIM)
                sum_ref[pl.ds(at, sub), cols] = (
                    sum_ref[pl.ds(at, sub), cols] * shrink + added[:, part : part + HEAD_DIM]
                )

    for n in range(chunks):

        @pl.when(jnp.logical_and(queries_real, counts[1 + n] >= depth))
        def _():
            attend(n, False)

        @pl.when(
            jnp.logical_and(
                queries_real, jnp.logical_and(counts[1 + n] > 0, counts[1 + n] < depth)
            )
        )
        def _():
            attend(n, True)

    if last:

        @pl.when(queries_real)
        def _():
            done = sum_ref[:, :HEAD_DIM] / sum_ref[:, HEAD_DIM:]
            out_ref[...] = done.astype(out_ref.dtype).reshape(out_ref.shape)

        @pl.when(jnp.logical_not(queries_real))
        def _():
            out_ref[...] = jnp.zeros_like(out_ref)


def attend_chunks(counts, qkv, pairs, carry, last, block=512, sub=256):
    sources, parts, tokens = qkv.shape[0], qkv.shape[1], qkv.shape[2]
    total = sources * tokens
    first = carry is None
    chunks = len(pairs) // 2

    def whole(array, part):
        if array.ndim == 4:
            return pl.BlockSpec(
                (sources, None, tokens, HEAD_DIM), lambda i, counts: (0, part, 0, 0)
            )
        return pl.BlockSpec((sources, tokens, HEAD_DIM), lambda i, counts: (0, 0, 0))

    in_specs = [
        pl.BlockSpec((block // tokens, None, tokens, HEAD_DIM), lambda i, counts: (i, 0, 0, 0))
    ]
    operands = [qkv]
    for array, part in pairs:
        in_specs.append(whole(array, part))
        operands.append(array)
    top_spec = pl.BlockSpec((block, HEAD_DIM), lambda i, counts: (i, 0))
    sum_spec = pl.BlockSpec((block, 2 * HEAD_DIM), lambda i, counts: (i, 0))
    if not first:
        in_specs += [top_spec, sum_spec]
        operands += list(carry)
    scratch = [pltpu.VMEM((chunks, total, 2 * HEAD_DIM), jnp.bfloat16)]
    if last:
        out_specs = pl.BlockSpec((block // tokens, tokens, HEAD_DIM), lambda i, counts: (i, 0, 0))
        out_shape = jax.ShapeDtypeStruct((sources, tokens, HEAD_DIM), jnp.bfloat16)
        scratch = [
            pltpu.VMEM((block, HEAD_DIM), jnp.float32),
            pltpu.VMEM((block, 2 * HEAD_DIM), jnp.float32),
        ] + scratch
    else:
        out_specs = [top_spec, sum_spec]
        out_shape = [
            jax.ShapeDtypeStruct((total, HEAD_DIM), jnp.float32),
            jax.ShapeDtypeStruct((total, 2 * HEAD_DIM), jnp.float32),
        ]

    def body(*refs):
        attention_kernel(first, last, chunks, sub, *refs)

    return pl.pallas_call(
        body,
        grid_spec=pltpu.PrefetchScalarGridSpec(
            num_scalar_prefetch=1,
            grid=(total // block,),
            in_specs=in_specs,
            out_specs=out_specs,
            scratch_shapes=scratch,
        ),
        out_shape=out_shape,
        cost_estimate=pl.CostEstimate(
            flops=8 * total * total * HEAD_DIM * chunks,
            bytes_accessed=4 << 20,
            transcendentals=total * total * chunks,
        ),
        compiler_params=pltpu.CompilerParams(vmem_limit_bytes=48 << 20),
        name="attend_last" if last else ("attend_first" if first else "attend_next"),
    )(counts, *operands)


def logits_kernel(blocks, tiles, counts, own_hbm, near_hbm, far_hbm, bias_ref, *refs):
    rows_in = refs[:blocks]
    slope_ref, total_ref, rows_ref, held, sems = refs[blocks:]
    step = pl.program_id(0)
    steps = pl.num_programs(0)
    cols = held.shape[2]

    def fetch(at, slot):
        def start(source, first):
            where = pl.ds(pl.multiple_of((at - first) * cols, cols), cols)
            pltpu.make_async_copy(source.at[:, where], held.at[slot], sems.at[slot]).start()

        @pl.when(at < tiles[0])
        def _():
            start(own_hbm, 0)

        @pl.when(jnp.logical_and(at >= tiles[0], at < tiles[1]))
        def _():
            start(near_hbm, tiles[0])

        @pl.when(at >= tiles[1])
        def _():
            start(far_hbm, tiles[1])

    slot = lax.rem(step, 2)

    @pl.when(step == 0)
    def _():
        fetch(step, slot)

    @pl.when(step + 1 < steps)
    def _():
        fetch(step + 1, 1 - slot)

    @pl.when(step == 0)
    def _():
        at = 0
        for ref in rows_in:
            rows_ref[pl.ds(at, ref.shape[0]), :] = ref[...]
            at += ref.shape[0]

    pltpu.make_async_copy(own_hbm.at[:, pl.ds(0, cols)], held.at[slot], sems.at[slot]).wait()
    logits = jnp.dot(rows_ref[...], held[slot], preferred_element_type=jnp.float32) + bias_ref[...]
    tokens = 64
    sums = [jnp.zeros((1, cols), jnp.float32), jnp.zeros((1, cols), jnp.float32)]
    for part in range(rows_ref.shape[0] // tokens):
        piece = logits[part * tokens : (part + 1) * tokens]
        base = 1.0 + jnp.maximum(piece, 0.0)
        power2 = base * base
        power4 = power2 * power2
        place = lax.broadcasted_iota(jnp.int32, piece.shape, 0)
        allowed = place < counts[part]
        boosted = jnp.where(allowed, power4 * power4, 0.0)
        slope = jnp.where(
            jnp.logical_and(allowed, piece > 0.0), power4 * (power2 * base), 0.0
        )
        slope_ref[pl.ds(part * tokens, tokens), :] = slope
        sums[part % 2] = sums[part % 2] + jnp.sum(boosted, axis=0, keepdims=True)
    total_ref[0:1, :] = sums[0]
    total_ref[1:2, :] = sums[1]


def boost(counts, weights, bias, blocks, cols=256):
    width = weights[0].shape[0]
    sizes = [w.shape[1] for w in weights]
    entries = sum(sizes)
    rows = sum(b.shape[0] for b in blocks)
    tiles = (sizes[0] // cols, (sizes[0] + sizes[1]) // cols)

    def body(*refs):
        logits_kernel(len(blocks), tiles, *refs)

    return pl.pallas_call(
        body,
        grid_spec=pltpu.PrefetchScalarGridSpec(
            num_scalar_prefetch=1,
            grid=(entries // cols,),
            in_specs=[pl.BlockSpec(memory_space=pl.ANY)] * 3
            + [pl.BlockSpec((1, cols), lambda j, counts: (0, j))]
            + [pl.BlockSpec(b.shape, lambda j, counts: (0, 0)) for b in blocks],
            out_specs=[
                pl.BlockSpec((rows, cols), lambda j, counts: (0, j)),
                pl.BlockSpec((2, cols), lambda j, counts: (0, j)),
            ],
            scratch_shapes=[
                pltpu.VMEM((rows, width), jnp.bfloat16),
                pltpu.VMEM((2, width, cols), jnp.bfloat16),
                pltpu.SemaphoreType.DMA((2,)),
            ],
        ),
        out_shape=[
            jax.ShapeDtypeStruct((rows, entries), jnp.float32),
            jax.ShapeDtypeStruct((2, entries), jnp.float32),
        ],
        cost_estimate=pl.CostEstimate(
            flops=4 * max(rows, 256) * width * entries,
            bytes_accessed=width * entries * 2 + rows * entries * 4,
            transcendentals=0,
        ),
        compiler_params=pltpu.CompilerParams(vmem_limit_bytes=40 << 20),
        name="boost",
    )(counts, *weights, bias, *blocks)


def gradient_kernel(outs, slope_ref, coef_ref, own_ref, near_ref, far_ref, *refs):
    out_refs, slopes = refs[:outs], refs[outs]
    tokens = 64

    @pl.when(pl.program_id(0) == 0)
    def _():
        for part in range(slopes.shape[0] // tokens):
            where = pl.ds(part * tokens, tokens)
            doc = part % 2
            slopes[where, :] = (coef_ref[doc : doc + 1, :] * slope_ref[where, :]).astype(
                slopes.dtype
            )

    result = None
    at = 0
    for ref in (own_ref, near_ref, far_ref):
        term = lax.dot_general(
            slopes[:, at : at + ref.shape[1]],
            ref[...],
            (((1,), (1,)), ((), ())),
            preferred_element_type=jnp.float32,
        )
        result = term if result is None else result + term
        at += ref.shape[1]
    at = 0
    for ref in out_refs:
        ref[...] = result[at : at + ref.shape[0]].astype(ref.dtype)
        at += ref.shape[0]


def gradient(slope, coefficient, weights, split, cols=256):
    rows, entries = slope.shape
    width = weights[0].shape[0]

    def body(*refs):
        gradient_kernel(len(split), *refs)

    return pl.pallas_call(
        body,
        grid=(width // cols,),
        in_specs=[
            pl.BlockSpec((rows, entries), lambda j: (0, 0)),
            pl.BlockSpec((2, entries), lambda j: (0, 0)),
        ]
        + [pl.BlockSpec((cols, w.shape[1]), lambda j: (j, 0)) for w in weights],
        out_specs=[pl.BlockSpec((n, cols), lambda j: (0, j)) for n in split],
        out_shape=[jax.ShapeDtypeStruct((n, width), jnp.bfloat16) for n in split],
        scratch_shapes=[pltpu.VMEM((rows, entries), jnp.bfloat16)],
        cost_estimate=pl.CostEstimate(
            flops=4 * max(rows, 256) * width * entries,
            bytes_accessed=width * entries * 2 + rows * entries * 4,
            transcendentals=0,
        ),
        compiler_params=pltpu.CompilerParams(vmem_limit_bytes=40 << 20),
        name="gradient",
    )(slope, coefficient, *weights)


def add(*terms):
    return sum(t.astype(jnp.float32) for t in terms).astype(jnp.bfloat16)


def local(
    queries, key_vectors, value_vectors, residual, norm_gain, head_weight, head_bias, doc_lengths
):
    tokens, docs, width = queries.shape
    heads = width // HEAD_DIM
    sizes = [lax.axis_size(axis) for axis in AXES]
    y_size, c_size, u_size, w_size, z_size = sizes
    plane = c_size * u_size * w_size * z_size
    y_at, c_at, u_at, w_at, z_at = [lax.axis_index(axis) for axis in AXES]

    def by_head(array):
        return jnp.transpose(array.reshape(tokens, docs, heads, HEAD_DIM), (1, 2, 0, 3)).reshape(
            docs * heads, tokens, HEAD_DIM
        )

    def move(array, **by):
        return lax.ppermute(array, AXES, shift_perm(sizes, **by))

    stacked = jnp.stack([by_head(a) for a in (queries, key_vectors, value_vectors)], axis=1)
    qkv = lax.all_to_all(stacked, PLANE, split_axis=0, concat_axis=0, tiled=True)
    block_rows = plane * tokens
    length = doc_lengths[c_at]

    def real(quarter):
        return jnp.clip(length - (quarter % y_size) * block_rows, 0, block_rows)

    mine = real(y_at)
    key_own, value_own = qkv[:, 1], qkv[:, 2]
    key_left = move(key_own, y=1)
    value_right = move(value_own, y=-1)
    value_left = move(value_own, y=1)
    key_right = move(key_own, y=-1)
    key_far = move(key_left, y=1)
    value_far = move(value_right, y=-1)

    entries = head_weight.shape[1]
    half = entries // 2
    late = (qkv[0, 0, 0, 0] > 100.0).astype(jnp.int32)
    near = move(lax.dynamic_slice_in_dim(head_weight, (c_at + late) * half, half, 1), u=1)
    far = move(near, c=1)
    weights = (head_weight, near, far)
    other_bias = move(head_bias.reshape(1, entries), u=1)

    def in_halves(array):
        swapped = jnp.concatenate([array[:, half:], array[:, :half]], axis=1)
        return jnp.where(c_at == 0, array, swapped)

    bias = jnp.concatenate([head_bias.reshape(1, entries), in_halves(other_bias)], axis=1)

    carry = attend_chunks(jnp.stack([mine, mine]), qkv, [(qkv, 1), (qkv, 2)], None, False)
    carry = attend_chunks(
        jnp.stack([mine, real(y_at - 1), real(y_at + 1)]),
        qkv,
        [(key_left, 0), (value_left, 0), (key_right, 0), (value_right, 0)],
        carry,
        False,
    )
    attended = attend_chunks(
        jnp.stack([mine, real(y_at + 2)]), qkv, [(key_far, 0), (value_far, 0)], carry, True
    )
    back = lax.all_to_all(attended, PLANE, split_axis=0, concat_axis=0, tiled=True)
    returned = jnp.transpose(back.reshape(docs, heads, tokens, HEAD_DIM), (0, 2, 1, 3)).reshape(
        docs * tokens, width
    )
    inward = jnp.transpose(residual, (1, 0, 2)).reshape(docs * tokens, width)
    combined = inward.astype(jnp.float32) + returned.astype(jnp.float32)
    inv_rms = lax.rsqrt(jnp.mean(combined * combined, axis=1, keepdims=True) + epsilon)
    hidden = (combined * inv_rms * norm_gain).astype(jnp.bfloat16)

    rows = {(0, 0): hidden}
    rows[1, 0] = move(hidden, w=1)
    rows[0, -1] = move(hidden, z=1)
    rows[0, 1] = move(hidden, z=-1)
    rows[1, -1] = move(rows[0, -1], w=1)
    rows[0, 2] = move(rows[0, -1], z=1)
    rows[1, 1] = move(rows[1, 0], z=-1)
    far_first = move(rows[1, -1][:tokens], z=1)
    far_second = move(rows[1, 1][tokens:], z=-1)

    def real_rows(places):
        counts = []
        for w_by, z_by in places:
            shard = (u_at * w_size + (w_at + w_by) % w_size) * z_size + (z_at + z_by) % z_size
            start = ((y_at * c_size + c_at) * u_size * w_size * z_size + shard) * tokens
            counts += [jnp.clip(doc_lengths[d] - start, 0, tokens) for d in range(docs)]
        return jnp.stack(counts)

    waves = [[(0, 0)], [(1, 0), (0, -1), (0, 1)], [(1, -1), (0, 2), (1, 1)], [(1, 2)]]
    slopes, sums = [], 0.0
    for wave in waves:
        blocks = [far_first, far_second] if wave == [(1, 2)] else [rows[at] for at in wave]
        slope, part = boost(real_rows(wave), weights, bias, blocks)
        slopes.append(slope)
        sums = sums + part

    own_sums, other_sums = sums[:, :entries], in_halves(sums[:, entries:])
    ordered = jnp.where(
        u_at == 0, jnp.stack([own_sums, other_sums]), jnp.stack([other_sums, own_sums])
    )
    peers = y_size * c_size * u_size
    spread = jnp.broadcast_to(ordered[None], (peers,) + ordered.shape)
    gathered = lax.all_to_all(spread, ("y", "c", "u"), split_axis=0, concat_axis=0, tiled=True)
    totals = jnp.sum(gathered, axis=0)
    pooled = jnp.log(totals / doc_lengths[None, :, None].astype(jnp.float32)) / sharpness
    coefficient = 2.0 * flops_weight / docs * jnp.mean(pooled, axis=1)[:, None, :] / totals
    own_pooled = jnp.where(u_at == 0, pooled[0], pooled[1])
    own_coef = jnp.where(u_at == 0, coefficient[0], coefficient[1])
    other_coef = in_halves(jnp.where(u_at == 0, coefficient[1], coefficient[0]))
    coef = jnp.concatenate([own_coef, other_coef], axis=1)

    block = docs * tokens
    first, second = gradient(slopes[3], coef, weights, [tokens, tokens])
    first = move(first, z=-1)
    second = move(second, z=1)
    left, across, right = gradient(slopes[2], coef, weights, [block] * 3)
    across = move(across, z=-1)
    left = jnp.concatenate([add(left[:tokens], first), left[tokens:]])
    right = jnp.concatenate([right[:tokens], add(right[tokens:], second)])
    left = move(left, w=1)
    right = move(right, z=1)
    pair, before, after = gradient(slopes[1], coef, weights, [block] * 3)
    after = move(after, z=1)
    pair = move(add(pair, right), w=1)
    before = move(add(before, left, across), z=-1)
    (own,) = gradient(slopes[0], coef, weights, [block])
    result = add(own, pair, before, after)
    return (own_pooled, jnp.transpose(result.reshape(docs, tokens, width), (1, 0, 2)))


def solution(mesh):
    grid = Mesh(mesh.devices.reshape(4, 2, 2, 2, 4), AXES)
    rows = P(AXES, None, None)
    vocab = ("u", "w", "z")
    in_specs = (rows, rows, rows, rows, P(), P(None, vocab), P(vocab), P())
    out_specs = (P(None, vocab), rows)
    return jax.shard_map(local, mesh=grid, in_specs=in_specs, out_specs=out_specs, check_vma=False)
```

```python
import math

import jax
import jax.numpy as jnp
from jax import lax
from jax.experimental import pallas as pl
from jax.experimental.pallas import tpu as pltpu
from jax.sharding import Mesh
from jax.sharding import PartitionSpec as P


HEAD_DIM = 128
AXES = ("y", "c", "u", "w", "z")
PLANE = ("c", "u", "w", "z")
LOW = -1e30

sharpness = 8.0
flops_weight = 500.0
epsilon = 1e-05


def shift_perm(sizes, **by):
    steps = [by.get(axis, 0) for axis in AXES]
    pairs = []
    for source in range(math.prod(sizes)):
        rest, place = source, []
        for size in reversed(sizes):
            place.append(rest % size)
            rest //= size
        target = 0
        for size, at, step in zip(sizes, reversed(place), steps):
            target = target * size + (at + step) % size
        pairs.append((source, target))
    return pairs


def attention_kernel(first, last, turns, sub, lengths, q_ref, *refs):
    chunks = len(turns)
    keys = refs[: 2 * chunks : 2]
    values = refs[1 : 2 * chunks : 2]
    rest = list(refs[2 * chunks :])
    if not first:
        top_in, sum_in = rest.pop(0), rest.pop(0)
    if last:
        out_ref = rest.pop(0)
        top_ref, sum_ref = rest.pop(0), rest.pop(0)
    else:
        top_ref, sum_ref = rest.pop(0), rest.pop(0)
    wide = rest.pop(0)
    step = pl.program_id(0)
    rows = top_ref.shape[0]
    depth = wide.shape[1]
    scale = math.log2(math.e) / math.sqrt(HEAD_DIM)

    @pl.when(step == 0)
    def _():
        for n in range(chunks):
            wide[n, :, :HEAD_DIM] = values[n][...].reshape(depth, HEAD_DIM)
            wide[n, :, HEAD_DIM:] = jnp.ones((depth, HEAD_DIM), wide.dtype)

    if first:
        top_ref[...] = jnp.full_like(top_ref, LOW)
        sum_ref[...] = jnp.zeros_like(sum_ref)
    else:
        top_ref[...] = top_in[...]
        sum_ref[...] = sum_in[...]
    length = lengths[lax.axis_index("c")]
    y_at, y_size = lax.axis_index("y"), lax.axis_size("y")
    queries_real = length - y_at * depth > step * rows
    counts = [length - lax.rem(y_at + turn + y_size, y_size) * depth for turn in turns]

    def attend(n, masked):
        key = keys[n][...].reshape(depth, HEAD_DIM)

        def piece(index, _):
            at = pl.multiple_of(index * sub, sub)
            query = q_ref[pl.ds(index * (sub // 64), sub // 64)].reshape(sub, HEAD_DIM)
            scores = lax.dot_general(
                query, key, (((1,), (1,)), ((), ())), preferred_element_type=jnp.float32
            )
            if masked:
                place = lax.broadcasted_iota(jnp.int32, scores.shape, 1)
                scores = jnp.where(place < counts[n], scores, LOW)
            old_top = top_ref[pl.ds(at, sub), :]
            new_top = jnp.maximum(old_top, jnp.max(scores, axis=1, keepdims=True))
            weights = jnp.exp2((scores - new_top[:, :1]) * scale)
            shrink = jnp.exp2((old_top - new_top) * scale)
            added = jnp.dot(
                weights.astype(jnp.bfloat16), wide[n], preferred_element_type=jnp.float32
            )
            top_ref[pl.ds(at, sub), :] = new_top
            for part in range(0, 2 * HEAD_DIM, HEAD_DIM):
                cols = pl.ds(part, HEAD_DIM)
                sum_ref[pl.ds(at, sub), cols] = (
                    sum_ref[pl.ds(at, sub), cols] * shrink + added[:, part : part + HEAD_DIM]
                )
            return 0

        lax.fori_loop(0, rows // sub, piece, 0)

    for n in range(chunks):

        @pl.when(jnp.logical_and(queries_real, counts[n] >= depth))
        def _():
            attend(n, False)

        @pl.when(
            jnp.logical_and(
                queries_real, jnp.logical_and(counts[n] > 0, counts[n] < depth)
            )
        )
        def _():
            attend(n, True)

    if last:

        @pl.when(queries_real)
        def _():
            done = sum_ref[:, :HEAD_DIM] / sum_ref[:, HEAD_DIM:]
            out_ref[...] = done.astype(out_ref.dtype).reshape(out_ref.shape)

        @pl.when(jnp.logical_not(queries_real))
        def _():
            out_ref[...] = jnp.zeros_like(out_ref)


def attend_chunks(lengths, qkv, pairs, turns, carry, last, block=512, sub=256):
    sources, tokens = qkv.shape[0], qkv.shape[2]
    total = sources * tokens
    first = carry is None
    chunks = len(pairs) // 2

    def whole(array, part):
        if array.ndim == 4:
            return pl.BlockSpec(
                (sources, None, tokens, HEAD_DIM), lambda i, counts: (0, part, 0, 0)
            )
        return pl.BlockSpec((sources, tokens, HEAD_DIM), lambda i, counts: (0, 0, 0))

    in_specs = [
        pl.BlockSpec((block // tokens, None, tokens, HEAD_DIM), lambda i, counts: (i, 0, 0, 0))
    ]
    operands = [qkv]
    for array, part in pairs:
        in_specs.append(whole(array, part))
        operands.append(array)
    top_spec = pl.BlockSpec((block, HEAD_DIM), lambda i, counts: (i, 0))
    sum_spec = pl.BlockSpec((block, 2 * HEAD_DIM), lambda i, counts: (i, 0))
    if not first:
        in_specs += [top_spec, sum_spec]
        operands += list(carry)
    scratch = [pltpu.VMEM((chunks, total, 2 * HEAD_DIM), jnp.bfloat16)]
    if last:
        out_specs = pl.BlockSpec((block // tokens, tokens, HEAD_DIM), lambda i, counts: (i, 0, 0))
        out_shape = jax.ShapeDtypeStruct((sources, tokens, HEAD_DIM), jnp.bfloat16)
        scratch = [
            pltpu.VMEM((block, HEAD_DIM), jnp.float32),
            pltpu.VMEM((block, 2 * HEAD_DIM), jnp.float32),
        ] + scratch
    else:
        out_specs = [top_spec, sum_spec]
        out_shape = [
            jax.ShapeDtypeStruct((total, HEAD_DIM), jnp.float32),
            jax.ShapeDtypeStruct((total, 2 * HEAD_DIM), jnp.float32),
        ]

    def body(*refs):
        attention_kernel(first, last, turns, sub, *refs)

    return pl.pallas_call(
        body,
        grid_spec=pltpu.PrefetchScalarGridSpec(
            num_scalar_prefetch=1,
            grid=(total // block,),
            in_specs=in_specs,
            out_specs=out_specs,
            scratch_shapes=scratch,
        ),
        out_shape=out_shape,
        cost_estimate=pl.CostEstimate(
            flops=8 * total * total * HEAD_DIM * chunks,
            bytes_accessed=4 << 20,
            transcendentals=total * total * chunks,
        ),
        compiler_params=pltpu.CompilerParams(vmem_limit_bytes=24 << 20),
        name="attend_last" if last else ("attend_first" if first else "attend_next"),
    )(lengths, *operands)


def logits_kernel(blocks, tiles, places, lengths, own_hbm, near_hbm, far_hbm, bias_ref, *refs):
    rows_in = refs[:blocks]
    slope_ref, total_ref, rows_ref, held, sems = refs[blocks:]
    step = pl.program_id(0)
    steps = pl.num_programs(0)
    cols = held.shape[2]

    def fetch(at, slot):
        def start(source, first):
            where = pl.ds(pl.multiple_of((at - first) * cols, cols), cols)
            pltpu.make_async_copy(source.at[:, where], held.at[slot], sems.at[slot]).start()

        @pl.when(at < tiles[0])
        def _():
            start(own_hbm, 0)

        @pl.when(jnp.logical_and(at >= tiles[0], at < tiles[1]))
        def _():
            start(near_hbm, tiles[0])

        @pl.when(at >= tiles[1])
        def _():
            start(far_hbm, tiles[1])

    slot = lax.rem(step, 2)

    @pl.when(step == 0)
    def _():
        fetch(step, slot)

    @pl.when(step + 1 < steps)
    def _():
        fetch(step + 1, 1 - slot)

    @pl.when(step == 0)
    def _():
        at = 0
        for ref in rows_in:
            rows_ref[pl.ds(at, ref.shape[0]), :] = ref[...]
            at += ref.shape[0]

    pltpu.make_async_copy(own_hbm.at[:, pl.ds(0, cols)], held.at[slot], sems.at[slot]).wait()
    logits = jnp.dot(rows_ref[...], held[slot], preferred_element_type=jnp.float32) + bias_ref[...]
    tokens = 64
    y_at, c_at, u_at, w_at, z_at = [lax.axis_index(axis) for axis in AXES]
    _, c_size, u_size, w_size, z_size = [lax.axis_size(axis) for axis in AXES]
    sums = [jnp.zeros((1, cols), jnp.float32), jnp.zeros((1, cols), jnp.float32)]
    for part in range(rows_ref.shape[0] // tokens):
        piece = logits[part * tokens : (part + 1) * tokens]
        base = 1.0 + jnp.maximum(piece, 0.0)
        power2 = base * base
        power4 = power2 * power2
        place = lax.broadcasted_iota(jnp.int32, piece.shape, 0)
        w_by, z_by = places[part // 2]
        shard = (y_at * c_size + c_at) * u_size + u_at
        shard = shard * w_size + lax.rem(w_at + w_by, w_size)
        shard = shard * z_size + lax.rem(z_at + z_by + z_size, z_size)
        allowed = place < lengths[part % 2] - shard * tokens
        boosted = jnp.where(allowed, power4 * power4, 0.0)
        slope = jnp.where(
            jnp.logical_and(allowed, piece > 0.0), power4 * (power2 * base), 0.0
        )
        slope_ref[pl.ds(part * tokens, tokens), :] = slope
        sums[part % 2] = sums[part % 2] + jnp.sum(boosted, axis=0, keepdims=True)
    total_ref[0:1, :] = sums[0]
    total_ref[1:2, :] = sums[1]


def boost(lengths, weights, bias, blocks, places, cols=256):
    width = weights[0].shape[0]
    sizes = [w.shape[1] for w in weights]
    entries = sum(sizes)
    rows = sum(b.shape[0] for b in blocks)
    tiles = (sizes[0] // cols, (sizes[0] + sizes[1]) // cols)

    def body(*refs):
        logits_kernel(len(blocks), tiles, places, *refs)

    return pl.pallas_call(
        body,
        grid_spec=pltpu.PrefetchScalarGridSpec(
            num_scalar_prefetch=1,
            grid=(entries // cols,),
            in_specs=[pl.BlockSpec(memory_space=pltpu.HBM)] * 3
            + [pl.BlockSpec((1, cols), lambda j, counts: (0, j))]
            + [pl.BlockSpec(b.shape, lambda j, counts: (0, 0)) for b in blocks],
            out_specs=[
                pl.BlockSpec((rows, cols), lambda j, counts: (0, j)),
                pl.BlockSpec((2, cols), lambda j, counts: (0, j)),
            ],
            scratch_shapes=[
                pltpu.VMEM((rows, width), jnp.bfloat16),
                pltpu.VMEM((2, width, cols), jnp.bfloat16),
                pltpu.SemaphoreType.DMA((2,)),
            ],
        ),
        out_shape=[
            pltpu.HBM((rows, entries), jnp.float32),
            jax.ShapeDtypeStruct((2, entries), jnp.float32),
        ],
        cost_estimate=pl.CostEstimate(
            flops=4 * max(rows, 256) * width * entries,
            bytes_accessed=width * entries * 2 + rows * entries * 4,
            transcendentals=0,
        ),
        compiler_params=pltpu.CompilerParams(vmem_limit_bytes=20 << 20),
        name="boost",
    )(lengths, *weights, bias, *blocks)


def gradient_kernel(outs, slope_ref, coef_ref, own_ref, near_ref, far_ref, *refs):
    out_refs, slopes = refs[:outs], refs[outs]
    tokens = 64

    @pl.when(pl.program_id(0) == 0)
    def _():
        for part in range(slopes.shape[0] // tokens):
            where = pl.ds(part * tokens, tokens)
            doc = part % 2
            slopes[where, :] = (coef_ref[doc : doc + 1, :] * slope_ref[where, :]).astype(
                slopes.dtype
            )

    result = None
    at = 0
    for ref in (own_ref, near_ref, far_ref):
        term = lax.dot_general(
            slopes[:, at : at + ref.shape[1]],
            ref[...],
            (((1,), (1,)), ((), ())),
            preferred_element_type=jnp.float32,
        )
        result = term if result is None else result + term
        at += ref.shape[1]
    at = 0
    for ref in out_refs:
        ref[...] = result[at : at + ref.shape[0]].astype(ref.dtype)
        at += ref.shape[0]


def gradient(slope, coefficient, weights, split, cols=256):
    rows, entries = slope.shape
    width = weights[0].shape[0]

    def body(*refs):
        gradient_kernel(len(split), *refs)

    return pl.pallas_call(
        body,
        grid=(width // cols,),
        in_specs=[
            pl.BlockSpec((rows, entries), lambda j: (0, 0)),
            pl.BlockSpec((2, entries), lambda j: (0, 0)),
        ]
        + [pl.BlockSpec((cols, w.shape[1]), lambda j: (j, 0)) for w in weights],
        out_specs=[pl.BlockSpec((n, cols), lambda j: (0, j)) for n in split],
        out_shape=[jax.ShapeDtypeStruct((n, width), jnp.bfloat16) for n in split],
        scratch_shapes=[pltpu.VMEM((rows, entries), jnp.bfloat16)],
        cost_estimate=pl.CostEstimate(
            flops=4 * max(rows, 256) * width * entries,
            bytes_accessed=width * entries * 2 + rows * entries * 4,
            transcendentals=0,
        ),
        compiler_params=pltpu.CompilerParams(vmem_limit_bytes=20 << 20),
        name="gradient",
    )(
        slope, coefficient, *[pltpu.with_memory_space_constraint(w, pltpu.HBM) for w in weights]
    )


def norm_kernel(docs, heads, back_ref, residual_ref, gain_ref, out_ref):
    tokens = residual_ref.shape[1]
    for d in range(docs):
        pieces = []
        squares = jnp.zeros((tokens, 1), jnp.float32)
        for h in range(heads):
            cols = slice(h * HEAD_DIM, (h + 1) * HEAD_DIM)
            piece = residual_ref[d, :, cols].astype(jnp.float32) + back_ref[d * heads + h].astype(
                jnp.float32
            )
            pieces.append(piece)
            squares = squares + jnp.sum(piece * piece, axis=1, keepdims=True)
        inv_rms = lax.rsqrt(squares / (heads * HEAD_DIM) + epsilon)
        for h in range(heads):
            cols = slice(h * HEAD_DIM, (h + 1) * HEAD_DIM)
            out_ref[d * tokens : (d + 1) * tokens, cols] = (
                pieces[h] * inv_rms * gain_ref[:, cols]
            ).astype(out_ref.dtype)


def normalized(back, residual, gain):
    docs, tokens, width = residual.shape
    return pl.pallas_call(
        lambda *refs: norm_kernel(docs, width // HEAD_DIM, *refs),
        out_shape=jax.ShapeDtypeStruct((docs * tokens, width), jnp.bfloat16),
        cost_estimate=pl.CostEstimate(
            flops=8 * docs * tokens * width, bytes_accessed=6 * docs * tokens * width, transcendentals=0
        ),
        compiler_params=pltpu.CompilerParams(vmem_limit_bytes=16 << 20),
        name="normalized",
    )(back, residual, gain.reshape(1, width))


def add(*terms):
    return sum(t.astype(jnp.float32) for t in terms).astype(jnp.bfloat16)


def local(
    queries, key_vectors, value_vectors, residual, norm_gain, head_weight, head_bias, doc_lengths
):
    tokens, docs, width = queries.shape
    heads = width // HEAD_DIM
    sizes = [lax.axis_size(axis) for axis in AXES]
    y_size, c_size, u_size, _, _ = sizes
    _, c_at, u_at, _, _ = [lax.axis_index(axis) for axis in AXES]

    def by_head(array):
        return jnp.transpose(array.reshape(tokens, docs, heads, HEAD_DIM), (1, 2, 0, 3)).reshape(
            docs * heads, tokens, HEAD_DIM
        )

    def move(array, **by):
        return lax.ppermute(array, AXES, shift_perm(sizes, **by))

    stacked = jnp.stack([by_head(a) for a in (queries, key_vectors, value_vectors)], axis=1)
    qkv = lax.all_to_all(stacked, PLANE, split_axis=0, concat_axis=0, tiled=True)
    key_own, value_own = qkv[:, 1], qkv[:, 2]
    key_left = move(key_own, y=1)
    value_right = move(value_own, y=-1)
    value_left = move(value_own, y=1)
    key_right = move(key_own, y=-1)
    key_far = move(key_left, y=1)
    value_far = move(value_right, y=-1)

    entries = head_weight.shape[1]
    half = entries // 2
    near = move(lax.dynamic_slice_in_dim(head_weight, c_at * half, half, 1), u=1)
    far = move(near, c=1)
    weights = (head_weight, near, far)
    other_bias = move(head_bias.reshape(1, entries), u=1)

    def in_halves(array):
        swapped = jnp.concatenate([array[:, half:], array[:, :half]], axis=1)
        return jnp.where(c_at == 0, array, swapped)

    bias = jnp.concatenate([head_bias.reshape(1, entries), in_halves(other_bias)], axis=1)

    carry = attend_chunks(doc_lengths, qkv, [(qkv, 1), (qkv, 2)], [0], None, False)
    carry = attend_chunks(
        doc_lengths,
        qkv,
        [(key_left, 0), (value_left, 0), (key_right, 0), (value_right, 0)],
        [-1, 1],
        carry,
        False,
    )
    attended = attend_chunks(
        doc_lengths, qkv, [(key_far, 0), (value_far, 0)], [2], carry, True
    )
    back = lax.all_to_all(attended, PLANE, split_axis=0, concat_axis=0, tiled=True)
    inward = jnp.transpose(residual, (1, 0, 2))
    hidden = normalized(back, inward, norm_gain)

    rows = {(0, 0): hidden}
    rows[1, 0] = move(hidden, w=1)
    rows[0, -1] = move(hidden, z=1)
    rows[0, 1] = move(hidden, z=-1)
    rows[1, -1] = move(rows[0, -1], w=1)
    rows[0, 2] = move(rows[0, -1], z=1)
    rows[1, 1] = move(rows[1, 0], z=-1)
    far_first = move(rows[1, -1][:tokens], z=1)
    far_second = move(rows[1, 1][tokens:], z=-1)

    waves = [[(0, 0)], [(1, 0), (0, -1), (0, 1)], [(1, -1), (0, 2), (1, 1)], [(1, 2)]]
    slopes, sums = [], 0.0
    for wave in waves:
        blocks = [far_first, far_second] if wave == [(1, 2)] else [rows[at] for at in wave]
        slope, part = boost(doc_lengths, weights, bias, blocks, wave)
        slopes.append(slope)
        sums = sums + part

    own_sums, other_sums = sums[:, :entries], in_halves(sums[:, entries:])
    ordered = jnp.where(
        u_at == 0, jnp.stack([own_sums, other_sums]), jnp.stack([other_sums, own_sums])
    )
    peers = y_size * c_size * u_size
    spread = jnp.broadcast_to(ordered[None], (peers,) + ordered.shape)
    gathered = lax.all_to_all(spread, ("y", "c", "u"), split_axis=0, concat_axis=0, tiled=True)
    totals = jnp.sum(gathered, axis=0)
    pooled = jnp.log(totals / doc_lengths[None, :, None].astype(jnp.float32)) / sharpness
    coefficient = 2.0 * flops_weight / docs * jnp.mean(pooled, axis=1)[:, None, :] / totals
    own_pooled = jnp.where(u_at == 0, pooled[0], pooled[1])
    own_coef = jnp.where(u_at == 0, coefficient[0], coefficient[1])
    other_coef = in_halves(jnp.where(u_at == 0, coefficient[1], coefficient[0]))
    coef = jnp.concatenate([own_coef, other_coef], axis=1)

    block = docs * tokens

    def terms(number, split):
        return gradient(slopes[number], coef, weights, split)

    first, second = terms(3, [tokens, tokens])
    first = move(first, z=-1)
    second = move(second, z=1)
    left, across, right = terms(2, [block] * 3)
    across = move(across, z=-1)
    left = jnp.concatenate([add(left[:tokens], first), left[tokens:]])
    right = jnp.concatenate([right[:tokens], add(right[tokens:], second)])
    left = move(left, w=1)
    right = move(right, z=1)
    pair, before, after = terms(1, [block] * 3)
    after = move(after, z=1)
    pair = move(add(pair, right), w=1)
    before = move(add(before, left, across), z=-1)
    (own,) = terms(0, [block])
    result = add(own, pair, before, after)
    return (own_pooled, jnp.transpose(result.reshape(docs, tokens, width), (1, 0, 2)))


def solution(mesh):
    grid = Mesh(mesh.devices.reshape(4, 2, 2, 2, 4), AXES)
    rows = P(AXES, None, None)
    vocab = ("u", "w", "z")
    in_specs = (rows, rows, rows, rows, P(), P(None, vocab), P(vocab), P())
    out_specs = (P(None, vocab), rows)

    return jax.shard_map(local, mesh=grid, in_specs=in_specs, out_specs=out_specs, check_vma=False)
```

```python
import math

import jax
import jax.numpy as jnp
from jax import lax
from jax.experimental import pallas as pl
from jax.experimental.pallas import tpu as pltpu
from jax.sharding import Mesh
from jax.sharding import PartitionSpec as P


HEAD_DIM = 128
AXES = ("y", "c", "u", "w", "z")
PLANE = ("c", "u", "w", "z")
LOW = -1e30

sharpness = 8.0
flops_weight = 500.0
epsilon = 1e-05


def shift_perm(sizes, **by):
    steps = [by.get(axis, 0) for axis in AXES]
    pairs = []
    for source in range(math.prod(sizes)):
        rest, place = source, []
        for size in reversed(sizes):
            place.append(rest % size)
            rest //= size
        target = 0
        for size, at, step in zip(sizes, reversed(place), steps):
            target = target * size + (at + step) % size
        pairs.append((source, target))
    return pairs


def attention_kernel(first, last, turns, sub, part, lengths, q_ref, *refs):
    chunks = len(turns)
    keys = refs[: 2 * chunks : 2]
    values = refs[1 : 2 * chunks : 2]
    rest = list(refs[2 * chunks :])
    if not first:
        top_in, sum_in = rest.pop(0), rest.pop(0)
    if last:
        out_ref = rest.pop(0)
        top_ref, sum_ref = rest.pop(0), rest.pop(0)
    else:
        top_ref, sum_ref = rest.pop(0), rest.pop(0)
    wide, held = rest.pop(0), rest.pop(0)
    step = pl.program_id(0)
    rows = top_ref.shape[0]
    depth = wide.shape[1]
    scale = math.log2(math.e) / math.sqrt(HEAD_DIM)

    @pl.when(step == 0)
    def _():
        for n in range(chunks):
            wide[n, :, :HEAD_DIM] = values[n][...].reshape(depth, HEAD_DIM)
            wide[n, :, HEAD_DIM:] = jnp.ones((depth, HEAD_DIM), wide.dtype)
            held[n] = keys[n][...].reshape(depth, HEAD_DIM)

    if first:
        top_ref[...] = jnp.full_like(top_ref, LOW)
        sum_ref[...] = jnp.zeros_like(sum_ref)
    else:
        top_ref[...] = top_in[...]
        sum_ref[...] = sum_in[...]
    length = lengths[lax.axis_index("c")]
    y_at, y_size = lax.axis_index("y"), lax.axis_size("y")
    queries_real = length - y_at * depth > step * rows

    def piece(n, at, count, masked):
        query = q_ref[pl.ds(at // 64, sub // 64)].reshape(sub, HEAD_DIM)
        where = pl.ds(at, sub)
        top = top_ref[where, :1]
        summed = sum_ref[where, :]
        for start in range(0, depth, part):
            key = held[n, start : start + part]
            scores = lax.dot_general(
                query, key, (((1,), (1,)), ((), ())), preferred_element_type=jnp.float32
            )
            if masked:
                place = lax.broadcasted_iota(jnp.int32, scores.shape, 1) + start
                scores = jnp.where(place < count, scores, LOW)
            new_top = jnp.maximum(top, jnp.max(scores, axis=1, keepdims=True))
            weights = jnp.exp2((scores - new_top) * scale)
            added = jnp.dot(
                weights.astype(jnp.bfloat16),
                wide[n, start : start + part],
                preferred_element_type=jnp.float32,
            )
            summed = summed * jnp.exp2((top - new_top) * scale) + added
            top = new_top
        top_ref[where, :] = jnp.broadcast_to(top, (sub, HEAD_DIM))
        sum_ref[where, :] = summed

    def attend(n, count, masked):
        if masked:

            def one(index, carry):
                piece(n, pl.multiple_of(index * sub, sub), count, True)
                return carry

            lax.fori_loop(0, rows // sub, one, 0)
        else:
            for at in range(0, rows, sub):
                piece(n, at, count, False)

    def chunk(n, carry):
        turn = turns[0] + n * (turns[-1] - turns[0])
        count = length - lax.rem(y_at + turn + y_size, y_size) * depth

        @pl.when(jnp.logical_and(queries_real, count >= depth))
        def _():
            attend(n, count, False)

        @pl.when(jnp.logical_and(queries_real, jnp.logical_and(count > 0, count < depth)))
        def _():
            attend(n, count, True)

        return carry

    if chunks == 1:
        chunk(0, 0)
    else:
        lax.fori_loop(0, chunks, chunk, 0)

    if last:

        @pl.when(queries_real)
        def _():
            done = sum_ref[:, :HEAD_DIM] / sum_ref[:, HEAD_DIM:]
            out_ref[...] = done.astype(out_ref.dtype).reshape(out_ref.shape)

        @pl.when(jnp.logical_not(queries_real))
        def _():
            out_ref[...] = jnp.zeros_like(out_ref)


def attend_chunks(lengths, qkv, pairs, turns, carry, last, block=512, sub=256, part=512):
    sources, tokens = qkv.shape[0], qkv.shape[2]
    total = sources * tokens
    first = carry is None
    chunks = len(pairs) // 2

    def whole(array, which):
        if array.ndim == 4:
            return pl.BlockSpec(
                (sources, None, tokens, HEAD_DIM), lambda i, counts: (0, which, 0, 0)
            )
        return pl.BlockSpec((sources, tokens, HEAD_DIM), lambda i, counts: (0, 0, 0))

    in_specs = [
        pl.BlockSpec((block // tokens, None, tokens, HEAD_DIM), lambda i, counts: (i, 0, 0, 0))
    ]
    operands = [qkv]
    for array, which in pairs:
        in_specs.append(whole(array, which))
        operands.append(array)
    top_spec = pl.BlockSpec((block, HEAD_DIM), lambda i, counts: (i, 0))
    sum_spec = pl.BlockSpec((block, 2 * HEAD_DIM), lambda i, counts: (i, 0))
    if not first:
        in_specs += [top_spec, sum_spec]
        operands += list(carry)
    scratch = [
        pltpu.VMEM((chunks, total, 2 * HEAD_DIM), jnp.bfloat16),
        pltpu.VMEM((chunks, total, HEAD_DIM), jnp.bfloat16),
    ]
    if last:
        out_specs = pl.BlockSpec((block // tokens, tokens, HEAD_DIM), lambda i, counts: (i, 0, 0))
        out_shape = jax.ShapeDtypeStruct((sources, tokens, HEAD_DIM), jnp.bfloat16)
        scratch = [
            pltpu.VMEM((block, HEAD_DIM), jnp.float32),
            pltpu.VMEM((block, 2 * HEAD_DIM), jnp.float32),
        ] + scratch
    else:
        out_specs = [top_spec, sum_spec]
        out_shape = [
            jax.ShapeDtypeStruct((total, HEAD_DIM), jnp.float32),
            jax.ShapeDtypeStruct((total, 2 * HEAD_DIM), jnp.float32),
        ]

    def body(*refs):
        attention_kernel(first, last, turns, sub, part, *refs)

    return pl.pallas_call(
        body,
        grid_spec=pltpu.PrefetchScalarGridSpec(
            num_scalar_prefetch=1,
            grid=(total // block,),
            in_specs=in_specs,
            out_specs=out_specs,
            scratch_shapes=scratch,
        ),
        out_shape=out_shape,
        cost_estimate=pl.CostEstimate(
            flops=8 * total * total * HEAD_DIM * chunks,
            bytes_accessed=4 << 20,
            transcendentals=total * total * chunks,
        ),
        compiler_params=pltpu.CompilerParams(vmem_limit_bytes=24 << 20),
        name="attend_last" if last else ("attend_first" if first else "attend_next"),
    )(lengths, *operands)


def logits_kernel(blocks, places, lengths, own_hbm, near_hbm, far_hbm, bias_ref, *refs):
    rows_in = refs[:blocks]
    slope_ref, total_ref, rows_ref, held, sems = refs[blocks:]
    step = pl.program_id(0)
    cols = held.shape[2]

    tile_sources = []
    for source in (own_hbm, near_hbm, far_hbm):
        tile_sources += [(source, at) for at in range(0, source.shape[1], cols)]

    @pl.when(step == 0)
    def _():
        for n, (source, at) in enumerate(tile_sources):
            pltpu.make_async_copy(
                source.at[:, at : at + cols], held.at[n], sems.at[n]
            ).start()

    @pl.when(step == 0)
    def _():
        at = 0
        for ref in rows_in:
            rows_ref[pl.ds(at, ref.shape[0]), :] = ref[...]
            at += ref.shape[0]

    pltpu.make_async_copy(own_hbm.at[:, pl.ds(0, cols)], held.at[step], sems.at[step]).wait()
    logits = jnp.dot(rows_ref[...], held[step], preferred_element_type=jnp.float32) + bias_ref[...]
    tokens = 64
    y_at, c_at, u_at, w_at, z_at = [lax.axis_index(axis) for axis in AXES]
    _, c_size, u_size, w_size, z_size = [lax.axis_size(axis) for axis in AXES]
    sums = [jnp.zeros((1, cols), jnp.float32), jnp.zeros((1, cols), jnp.float32)]
    for part in range(rows_ref.shape[0] // tokens):
        piece = logits[part * tokens : (part + 1) * tokens]
        base = 1.0 + jnp.maximum(piece, 0.0)
        power2 = base * base
        power4 = power2 * power2
        place = lax.broadcasted_iota(jnp.int32, piece.shape, 0)
        w_by, z_by = places[part // 2]
        shard = (y_at * c_size + c_at) * u_size + u_at
        shard = shard * w_size + lax.rem(w_at + w_by, w_size)
        shard = shard * z_size + lax.rem(z_at + z_by + z_size, z_size)
        allowed = place < lengths[part % 2] - shard * tokens
        boosted = jnp.where(allowed, power4 * power4, 0.0)
        slope = jnp.where(
            jnp.logical_and(allowed, piece > 0.0), power4 * (power2 * base), 0.0
        )
        slope_ref[pl.ds(part * tokens, tokens), :] = slope
        sums[part % 2] = sums[part % 2] + jnp.sum(boosted, axis=0, keepdims=True)
    total_ref[0:1, :] = sums[0]
    total_ref[1:2, :] = sums[1]


def boost(lengths, weights, bias, blocks, places, cols=256):
    width = weights[0].shape[0]
    sizes = [w.shape[1] for w in weights]
    entries = sum(sizes)
    rows = sum(b.shape[0] for b in blocks)
    tiles = entries // cols

    def body(*refs):
        logits_kernel(len(blocks), places, *refs)

    return pl.pallas_call(
        body,
        grid_spec=pltpu.PrefetchScalarGridSpec(
            num_scalar_prefetch=1,
            grid=(tiles,),
            in_specs=[pl.BlockSpec(memory_space=pltpu.HBM)] * 3
            + [pl.BlockSpec((1, cols), lambda j, counts: (0, j))]
            + [pl.BlockSpec(b.shape, lambda j, counts: (0, 0)) for b in blocks],
            out_specs=[
                pl.BlockSpec((rows, cols), lambda j, counts: (0, j)),
                pl.BlockSpec((2, cols), lambda j, counts: (0, j)),
            ],
            scratch_shapes=[
                pltpu.VMEM((rows, width), jnp.bfloat16),
                pltpu.VMEM((tiles, width, cols), jnp.bfloat16),
                pltpu.SemaphoreType.DMA((tiles,)),
            ],
        ),
        out_shape=[
            pltpu.HBM((rows, entries), jnp.float32),
            jax.ShapeDtypeStruct((2, entries), jnp.float32),
        ],
        cost_estimate=pl.CostEstimate(
            flops=4 * max(rows, 256) * width * entries,
            bytes_accessed=width * entries * 2 + rows * entries * 4,
            transcendentals=0,
        ),
        compiler_params=pltpu.CompilerParams(vmem_limit_bytes=28 << 20),
        name="boost",
    )(lengths, *weights, bias, *blocks)


def gradient_kernel(outs, slope_ref, coef_ref, own_hbm, near_hbm, far_hbm, *refs):
    out_refs, slopes, held, sems = refs[:outs], *refs[outs:]
    tokens = 64
    step = pl.program_id(0)
    tiles, cols = held.shape[0], held.shape[1]
    sources = (own_hbm, near_hbm, far_hbm)

    def copies(tile, feature):
        at = 0
        for n, source in enumerate(sources):
            yield pltpu.make_async_copy(
                source.at[pl.ds(feature, cols), :],
                held.at[tile, :, at : at + source.shape[1]],
                sems.at[tile, n],
            )
            at += source.shape[1]

    @pl.when(step == 0)
    def _():
        for tile in range(tiles):
            for copy in copies(tile, tile * cols):
                copy.start()
        for part in range(slopes.shape[0] // tokens):
            where = pl.ds(part * tokens, tokens)
            doc = part % 2
            slopes[where, :] = (coef_ref[doc : doc + 1, :] * slope_ref[where, :]).astype(
                slopes.dtype
            )

    for copy in copies(step, 0):
        copy.wait()
    result = lax.dot_general(
        slopes[...], held[step], (((1,), (1,)), ((), ())), preferred_element_type=jnp.float32
    )
    at = 0
    for ref in out_refs:
        ref[...] = result[at : at + ref.shape[0]].astype(ref.dtype)
        at += ref.shape[0]


def gradient(slope, coefficient, weights, split, cols=256):
    rows, entries = slope.shape
    width = weights[0].shape[0]

    def body(*refs):
        gradient_kernel(len(split), *refs)

    return pl.pallas_call(
        body,
        grid=(width // cols,),
        in_specs=[
            pl.BlockSpec((rows, entries), lambda j: (0, 0)),
            pl.BlockSpec((2, entries), lambda j: (0, 0)),
        ]
        + [pl.BlockSpec(memory_space=pltpu.HBM)] * 3,
        out_specs=[pl.BlockSpec((n, cols), lambda j: (0, j)) for n in split],
        out_shape=[jax.ShapeDtypeStruct((n, width), jnp.bfloat16) for n in split],
        scratch_shapes=[
            pltpu.VMEM((rows, entries), jnp.bfloat16),
            pltpu.VMEM((width // cols, cols, entries), jnp.bfloat16),
            pltpu.SemaphoreType.DMA((width // cols, 3)),
        ],
        cost_estimate=pl.CostEstimate(
            flops=4 * max(rows, 256) * width * entries,
            bytes_accessed=width * entries * 2 + rows * entries * 4,
            transcendentals=0,
        ),
        compiler_params=pltpu.CompilerParams(vmem_limit_bytes=28 << 20),
        name="gradient",
    )(slope, coefficient, *weights)


def norm_kernel(docs, heads, back_ref, residual_ref, gain_ref, out_ref):
    tokens = residual_ref.shape[1]
    for d in range(docs):
        pieces = []
        squares = jnp.zeros((tokens, 1), jnp.float32)
        for h in range(heads):
            cols = slice(h * HEAD_DIM, (h + 1) * HEAD_DIM)
            piece = residual_ref[d, :, cols].astype(jnp.float32) + back_ref[d * heads + h].astype(
                jnp.float32
            )
            pieces.append(piece)
            squares = squares + jnp.sum(piece * piece, axis=1, keepdims=True)
        inv_rms = lax.rsqrt(squares / (heads * HEAD_DIM) + epsilon)
        for h in range(heads):
            cols = slice(h * HEAD_DIM, (h + 1) * HEAD_DIM)
            out_ref[d * tokens : (d + 1) * tokens, cols] = (
                pieces[h] * inv_rms * gain_ref[:, cols]
            ).astype(out_ref.dtype)


def normalized(back, residual, gain):
    docs, tokens, width = residual.shape
    return pl.pallas_call(
        lambda *refs: norm_kernel(docs, width // HEAD_DIM, *refs),
        out_shape=jax.ShapeDtypeStruct((docs * tokens, width), jnp.bfloat16),
        cost_estimate=pl.CostEstimate(
            flops=8 * docs * tokens * width, bytes_accessed=6 * docs * tokens * width, transcendentals=0
        ),
        compiler_params=pltpu.CompilerParams(vmem_limit_bytes=16 << 20),
        name="normalized",
    )(back, residual, gain.reshape(1, width))


def add(*terms):
    return sum(t.astype(jnp.float32) for t in terms).astype(jnp.bfloat16)


def local(
    queries, key_vectors, value_vectors, residual, norm_gain, head_weight, head_bias, doc_lengths
):
    tokens, docs, width = queries.shape
    heads = width // HEAD_DIM
    sizes = [lax.axis_size(axis) for axis in AXES]
    y_size, c_size, u_size, _, _ = sizes
    _, c_at, u_at, _, _ = [lax.axis_index(axis) for axis in AXES]

    def by_head(array):
        return jnp.transpose(array.reshape(tokens, docs, heads, HEAD_DIM), (1, 2, 0, 3)).reshape(
            docs * heads, tokens, HEAD_DIM
        )

    def move(array, **by):
        return lax.ppermute(array, AXES, shift_perm(sizes, **by))

    stacked = jnp.stack([by_head(a) for a in (queries, key_vectors, value_vectors)], axis=1)
    qkv = lax.all_to_all(stacked, PLANE, split_axis=0, concat_axis=0, tiled=True)
    key_own, value_own = qkv[:, 1], qkv[:, 2]
    key_left = move(key_own, y=1)
    value_right = move(value_own, y=-1)
    value_left = move(value_own, y=1)
    key_right = move(key_own, y=-1)
    key_far = move(key_left, y=1)
    value_far = move(value_right, y=-1)

    entries = head_weight.shape[1]
    half = entries // 2
    near = move(lax.dynamic_slice_in_dim(head_weight, c_at * half, half, 1), u=1)
    far = move(near, c=1)
    weights = (head_weight, near, far)
    other_bias = move(head_bias.reshape(1, entries), u=1)

    def in_halves(array):
        swapped = jnp.concatenate([array[:, half:], array[:, :half]], axis=1)
        return jnp.where(c_at == 0, array, swapped)

    bias = jnp.concatenate([head_bias.reshape(1, entries), in_halves(other_bias)], axis=1)

    carry = attend_chunks(doc_lengths, qkv, [(qkv, 1), (qkv, 2)], [0], None, False)
    carry = attend_chunks(
        doc_lengths,
        qkv,
        [(key_left, 0), (value_left, 0), (key_right, 0), (value_right, 0)],
        [-1, 1],
        carry,
        False,
    )
    attended = attend_chunks(
        doc_lengths, qkv, [(key_far, 0), (value_far, 0)], [2], carry, True
    )
    back = lax.all_to_all(attended, PLANE, split_axis=0, concat_axis=0, tiled=True)
    inward = jnp.transpose(residual, (1, 0, 2))
    hidden = normalized(back, inward, norm_gain)

    rows = {(0, 0): hidden}
    rows[1, 0] = move(hidden, w=1)
    rows[0, -1] = move(hidden, z=1)
    rows[0, 1] = move(hidden, z=-1)
    rows[1, -1] = move(rows[0, -1], w=1)
    rows[0, 2] = move(rows[0, -1], z=1)
    rows[1, 1] = move(rows[1, 0], z=-1)
    far_first = move(rows[1, -1][:tokens], z=1)
    far_second = move(rows[1, 1][tokens:], z=-1)

    waves = [[(0, 0)], [(1, 0), (0, -1), (0, 1)], [(1, -1), (0, 2), (1, 1)], [(1, 2)]]
    slopes, sums = [], 0.0
    for wave in waves:
        blocks = [far_first, far_second] if wave == [(1, 2)] else [rows[at] for at in wave]
        slope, part = boost(doc_lengths, weights, bias, blocks, wave)
        slopes.append(slope)
        sums = sums + part

    own_sums, other_sums = sums[:, :entries], in_halves(sums[:, entries:])
    ordered = jnp.where(
        u_at == 0, jnp.stack([own_sums, other_sums]), jnp.stack([other_sums, own_sums])
    )
    peers = y_size * c_size * u_size
    spread = jnp.broadcast_to(ordered[None], (peers,) + ordered.shape)
    gathered = lax.all_to_all(spread, ("y", "c", "u"), split_axis=0, concat_axis=0, tiled=True)
    totals = jnp.sum(gathered, axis=0)
    pooled = jnp.log(totals / doc_lengths[None, :, None].astype(jnp.float32)) / sharpness
    coefficient = 2.0 * flops_weight / docs * jnp.mean(pooled, axis=1)[:, None, :] / totals
    own_pooled = jnp.where(u_at == 0, pooled[0], pooled[1])
    own_coef = jnp.where(u_at == 0, coefficient[0], coefficient[1])
    other_coef = in_halves(jnp.where(u_at == 0, coefficient[1], coefficient[0]))
    coef = jnp.concatenate([own_coef, other_coef], axis=1)

    block = docs * tokens

    def terms(number, split):
        return gradient(slopes[number], coef, weights, split)

    first, second = terms(3, [tokens, tokens])
    first = move(first, z=-1)
    second = move(second, z=1)
    left, across, right = terms(2, [block] * 3)
    across = move(across, z=-1)
    left = jnp.concatenate([add(left[:tokens], first), left[tokens:]])
    right = jnp.concatenate([right[:tokens], add(right[tokens:], second)])
    left = move(left, w=1)
    right = move(right, z=1)
    pair, before, after = terms(1, [block] * 3)
    after = move(after, z=1)
    pair = move(add(pair, right), w=1)
    before = move(add(before, left, across), z=-1)
    (own,) = terms(0, [block])
    result = add(own, pair, before, after)
    return (own_pooled, jnp.transpose(result.reshape(docs, tokens, width), (1, 0, 2)))


def solution(mesh):
    grid = Mesh(mesh.devices.reshape(4, 2, 2, 2, 4), AXES)
    rows = P(AXES, None, None)
    vocab = ("u", "w", "z")
    in_specs = (rows, rows, rows, rows, P(), P(None, vocab), P(vocab), P())
    out_specs = (P(None, vocab), rows)

    return jax.shard_map(local, mesh=grid, in_specs=in_specs, out_specs=out_specs, check_vma=False)
```

```python
import math

import jax
import jax.numpy as jnp
from jax import lax
from jax.experimental import pallas as pl
from jax.experimental.pallas import tpu as pltpu
from jax.sharding import Mesh
from jax.sharding import PartitionSpec as P


HEAD_DIM = 128
AXES = ("y", "c", "u", "w", "z")
PLANE = ("c", "u", "w", "z")
LOW = -1e30

sharpness = 8.0
flops_weight = 500.0
epsilon = 1e-05


def shift_perm(sizes, **by):
    steps = [by.get(axis, 0) for axis in AXES]
    pairs = []
    for source in range(math.prod(sizes)):
        rest, place = source, []
        for size in reversed(sizes):
            place.append(rest % size)
            rest //= size
        target = 0
        for size, at, step in zip(sizes, reversed(place), steps):
            target = target * size + (at + step) % size
        pairs.append((source, target))
    return pairs


def attention_kernel(first, last, turns, sub, part, lengths, q_ref, *refs):
    chunks = len(turns)
    keys = refs[: 2 * chunks : 2]
    values = refs[1 : 2 * chunks : 2]
    rest = list(refs[2 * chunks :])
    if not first:
        top_in, sum_in = rest.pop(0), rest.pop(0)
    if last:
        out_ref = rest.pop(0)
        top_ref, sum_ref = rest.pop(0), rest.pop(0)
    else:
        top_ref, sum_ref = rest.pop(0), rest.pop(0)
    wide, held = rest.pop(0), rest.pop(0)
    step = pl.program_id(0)
    rows = top_ref.shape[0]
    depth = wide.shape[1]
    scale = math.log2(math.e) / math.sqrt(HEAD_DIM)

    @pl.when(step == 0)
    def _():
        for n in range(chunks):
            wide[n, :, :HEAD_DIM] = values[n][...].reshape(depth, HEAD_DIM)
            wide[n, :, HEAD_DIM:] = jnp.ones((depth, HEAD_DIM), wide.dtype)
            held[n] = keys[n][...].reshape(depth, HEAD_DIM)

    if first:
        top_ref[...] = jnp.full_like(top_ref, LOW)
        sum_ref[...] = jnp.zeros_like(sum_ref)
    else:
        top_ref[...] = top_in[...]
        sum_ref[...] = sum_in[...]
    length = lengths[lax.axis_index("c")]
    y_at, y_size = lax.axis_index("y"), lax.axis_size("y")
    queries_real = length - y_at * depth > step * rows

    def piece(n, at, count, masked, top, summed):
        query = q_ref[pl.ds(at // 64, sub // 64)].reshape(sub, HEAD_DIM)
        for start in range(0, depth, part):
            key = held[n, start : start + part]
            scores = lax.dot_general(
                query, key, (((1,), (1,)), ((), ())), preferred_element_type=jnp.float32
            )
            if masked:
                place = lax.broadcasted_iota(jnp.int32, scores.shape, 1) + start
                scores = jnp.where(place < count, scores, LOW)
            new_top = jnp.max(scores, axis=1, keepdims=True)
            if top is not None:
                new_top = jnp.maximum(top, new_top)
            weights = jnp.exp2((scores - new_top) * scale)
            added = jnp.dot(
                weights.astype(jnp.bfloat16),
                wide[n, start : start + part],
                preferred_element_type=jnp.float32,
            )
            if top is not None:
                added = summed * jnp.exp2((top - new_top) * scale) + added
            top, summed = new_top, added
        return top, summed

    def before(at):
        return (None, None) if first else (top_ref[pl.ds(at, sub), :1], sum_ref[pl.ds(at, sub), :])

    def after(at, top, summed):
        top_ref[pl.ds(at, sub), :] = jnp.broadcast_to(top, (sub, HEAD_DIM))
        sum_ref[pl.ds(at, sub), :] = summed

    def attend(n, count, masked):
        if masked:

            def one(index, carry):
                at = pl.multiple_of(index * sub, sub)
                after(at, *piece(n, at, count, True, *before(at)))
                return carry

            lax.fori_loop(0, rows // sub, one, 0)
        else:
            places = range(0, rows, sub)
            running = [before(at) for at in places]
            done = [piece(n, at, count, False, *run) for at, run in zip(places, running)]
            for at, run in zip(places, done):
                after(at, *run)

    def chunk(n, carry):
        turn = turns[0] + n * (turns[-1] - turns[0])
        count = length - lax.rem(y_at + turn + y_size, y_size) * depth

        @pl.when(jnp.logical_and(queries_real, count >= depth))
        def _():
            attend(n, count, False)

        @pl.when(jnp.logical_and(queries_real, jnp.logical_and(count > 0, count < depth)))
        def _():
            attend(n, count, True)

        return carry

    if chunks == 1:
        chunk(0, 0)
    else:
        lax.fori_loop(0, chunks, chunk, 0)

    if last:

        @pl.when(queries_real)
        def _():
            done = sum_ref[:, :HEAD_DIM] / sum_ref[:, HEAD_DIM:]
            out_ref[...] = done.astype(out_ref.dtype).reshape(out_ref.shape)

        @pl.when(jnp.logical_not(queries_real))
        def _():
            out_ref[...] = jnp.zeros_like(out_ref)


def attend_chunks(lengths, qkv, pairs, turns, carry, last, block=512, sub=256, part=512):
    sources, tokens = qkv.shape[0], qkv.shape[2]
    total = sources * tokens
    first = carry is None
    chunks = len(pairs) // 2

    def whole(array, which):
        if array.ndim == 4:
            return pl.BlockSpec(
                (sources, None, tokens, HEAD_DIM), lambda i, counts: (0, which, 0, 0)
            )
        return pl.BlockSpec((sources, tokens, HEAD_DIM), lambda i, counts: (0, 0, 0))

    in_specs = [
        pl.BlockSpec((block // tokens, None, tokens, HEAD_DIM), lambda i, counts: (i, 0, 0, 0))
    ]
    operands = [qkv]
    for array, which in pairs:
        in_specs.append(whole(array, which))
        operands.append(array)
    top_spec = pl.BlockSpec((block, HEAD_DIM), lambda i, counts: (i, 0))
    sum_spec = pl.BlockSpec((block, 2 * HEAD_DIM), lambda i, counts: (i, 0))
    if not first:
        in_specs += [top_spec, sum_spec]
        operands += list(carry)
    scratch = [
        pltpu.VMEM((chunks, total, 2 * HEAD_DIM), jnp.bfloat16),
        pltpu.VMEM((chunks, total, HEAD_DIM), jnp.bfloat16),
    ]
    if last:
        out_specs = pl.BlockSpec((block // tokens, tokens, HEAD_DIM), lambda i, counts: (i, 0, 0))
        out_shape = jax.ShapeDtypeStruct((sources, tokens, HEAD_DIM), jnp.bfloat16)
        scratch = [
            pltpu.VMEM((block, HEAD_DIM), jnp.float32),
            pltpu.VMEM((block, 2 * HEAD_DIM), jnp.float32),
        ] + scratch
    else:
        out_specs = [top_spec, sum_spec]
        out_shape = [
            jax.ShapeDtypeStruct((total, HEAD_DIM), jnp.float32),
            jax.ShapeDtypeStruct((total, 2 * HEAD_DIM), jnp.float32),
        ]

    def body(*refs):
        attention_kernel(first, last, turns, sub, part, *refs)

    return pl.pallas_call(
        body,
        grid_spec=pltpu.PrefetchScalarGridSpec(
            num_scalar_prefetch=1,
            grid=(total // block,),
            in_specs=in_specs,
            out_specs=out_specs,
            scratch_shapes=scratch,
        ),
        out_shape=out_shape,
        cost_estimate=pl.CostEstimate(
            flops=8 * total * total * HEAD_DIM * chunks,
            bytes_accessed=4 << 20,
            transcendentals=total * total * chunks,
        ),
        compiler_params=pltpu.CompilerParams(vmem_limit_bytes=24 << 20),
        name="attend_last" if last else ("attend_first" if first else "attend_next"),
    )(lengths, *operands)


def logits_kernel(blocks, places, cols, lengths, own_ref, near_ref, far_ref, bias_ref, *refs):
    rows_in = refs[:blocks]
    slope_ref, total_ref, rows_ref, logits_ref = refs[blocks:]
    step = pl.program_id(0)

    @pl.when(step == 0)
    def _():
        at = 0
        for ref in rows_in:
            rows_ref[pl.ds(at, ref.shape[0]), :] = ref[...]
            at += ref.shape[0]

    first = 0
    for ref in (own_ref, near_ref, far_ref):
        tiles = ref.shape[1] // cols

        @pl.when(jnp.logical_and(step >= first, step < first + tiles))
        def _():
            where = pl.ds(pl.multiple_of((step - first) * cols, cols), cols)
            logits_ref[...] = jnp.dot(
                rows_ref[...], ref[:, where], preferred_element_type=jnp.float32
            )

        first += tiles
    logits = logits_ref[...] + bias_ref[...]
    tokens = 64
    y_at, c_at, u_at, w_at, z_at = [lax.axis_index(axis) for axis in AXES]
    _, c_size, u_size, w_size, z_size = [lax.axis_size(axis) for axis in AXES]
    sums = [jnp.zeros((1, cols), jnp.float32), jnp.zeros((1, cols), jnp.float32)]
    for part in range(rows_ref.shape[0] // tokens):
        piece = logits[part * tokens : (part + 1) * tokens]
        base = 1.0 + jnp.maximum(piece, 0.0)
        power2 = base * base
        power4 = power2 * power2
        place = lax.broadcasted_iota(jnp.int32, piece.shape, 0)
        w_by, z_by = places[part // 2]
        shard = (y_at * c_size + c_at) * u_size + u_at
        shard = shard * w_size + lax.rem(w_at + w_by, w_size)
        shard = shard * z_size + lax.rem(z_at + z_by + z_size, z_size)
        allowed = place < lengths[part % 2] - shard * tokens
        boosted = jnp.where(allowed, power4 * power4, 0.0)
        slope = jnp.where(
            jnp.logical_and(allowed, piece > 0.0), power4 * (power2 * base), 0.0
        )
        slope_ref[pl.ds(part * tokens, tokens), :] = slope
        sums[part % 2] = sums[part % 2] + jnp.sum(boosted, axis=0, keepdims=True)
    total_ref[0:1, :] = sums[0]
    total_ref[1:2, :] = sums[1]


def boost(lengths, weights, bias, blocks, places, cols=256):
    width = weights[0].shape[0]
    sizes = [w.shape[1] for w in weights]
    entries = sum(sizes)
    rows = sum(b.shape[0] for b in blocks)
    tiles = entries // cols

    def body(*refs):
        logits_kernel(len(blocks), places, cols, *refs)

    return pl.pallas_call(
        body,
        grid_spec=pltpu.PrefetchScalarGridSpec(
            num_scalar_prefetch=1,
            grid=(tiles,),
            in_specs=[pl.BlockSpec(memory_space=pltpu.VMEM)] * 3
            + [pl.BlockSpec((1, cols), lambda j, counts: (0, j))]
            + [pl.BlockSpec(b.shape, lambda j, counts: (0, 0)) for b in blocks],
            out_specs=[
                pl.BlockSpec((rows, cols), lambda j, counts: (0, j)),
                pl.BlockSpec((2, cols), lambda j, counts: (0, j)),
            ],
            scratch_shapes=[
                pltpu.VMEM((rows, width), jnp.bfloat16),
                pltpu.VMEM((rows, cols), jnp.float32),
            ],
        ),
        out_shape=[
            pltpu.HBM((rows, entries), jnp.float32),
            jax.ShapeDtypeStruct((2, entries), jnp.float32),
        ],
        cost_estimate=pl.CostEstimate(
            flops=4 * max(rows, 256) * width * entries,
            bytes_accessed=width * entries * 2 + rows * entries * 4,
            transcendentals=0,
        ),
        compiler_params=pltpu.CompilerParams(vmem_limit_bytes=28 << 20),
        name="boost",
    )(lengths, *weights, bias, *blocks)


def gradient_kernel(outs, slope_ref, coef_ref, own_hbm, near_hbm, far_hbm, *refs):
    out_refs, slopes, held, sems = refs[:outs], *refs[outs:]
    tokens = 64
    step = pl.program_id(0)
    tiles, cols = held.shape[0], held.shape[1]
    sources = (own_hbm, near_hbm, far_hbm)

    def copies(tile, feature):
        at = 0
        for n, source in enumerate(sources):
            yield pltpu.make_async_copy(
                source.at[pl.ds(feature, cols), :],
                held.at[tile, :, at : at + source.shape[1]],
                sems.at[tile, n],
            )
            at += source.shape[1]

    @pl.when(step == 0)
    def _():
        for tile in range(tiles):
            for copy in copies(tile, tile * cols):
                copy.start()
        for part in range(slopes.shape[0] // tokens):
            where = pl.ds(part * tokens, tokens)
            doc = part % 2
            slopes[where, :] = (coef_ref[doc : doc + 1, :] * slope_ref[where, :]).astype(
                slopes.dtype
            )

    for copy in copies(step, 0):
        copy.wait()
    result = lax.dot_general(
        slopes[...], held[step], (((1,), (1,)), ((), ())), preferred_element_type=jnp.float32
    )
    at = 0
    for ref in out_refs:
        ref[...] = result[at : at + ref.shape[0]].astype(ref.dtype)
        at += ref.shape[0]


def gradient(slope, coefficient, weights, split, cols=256):
    rows, entries = slope.shape
    width = weights[0].shape[0]

    def body(*refs):
        gradient_kernel(len(split), *refs)

    return pl.pallas_call(
        body,
        grid=(width // cols,),
        in_specs=[
            pl.BlockSpec((rows, entries), lambda j: (0, 0)),
            pl.BlockSpec((2, entries), lambda j: (0, 0)),
        ]
        + [pl.BlockSpec(memory_space=pltpu.HBM)] * 3,
        out_specs=[pl.BlockSpec((n, cols), lambda j: (0, j)) for n in split],
        out_shape=[jax.ShapeDtypeStruct((n, width), jnp.bfloat16) for n in split],
        scratch_shapes=[
            pltpu.VMEM((rows, entries), jnp.bfloat16),
            pltpu.VMEM((width // cols, cols, entries), jnp.bfloat16),
            pltpu.SemaphoreType.DMA((width // cols, 3)),
        ],
        cost_estimate=pl.CostEstimate(
            flops=4 * max(rows, 256) * width * entries,
            bytes_accessed=width * entries * 2 + rows * entries * 4,
            transcendentals=0,
        ),
        compiler_params=pltpu.CompilerParams(vmem_limit_bytes=28 << 20),
        name="gradient",
    )(
        pltpu.with_memory_space_constraint(slope, pltpu.HBM),
        coefficient,
        *[pltpu.with_memory_space_constraint(w, pltpu.HBM) for w in weights],
    )


def norm_kernel(docs, heads, back_ref, residual_ref, gain_ref, out_ref):
    tokens = residual_ref.shape[1]
    for d in range(docs):
        pieces = []
        squares = jnp.zeros((tokens, 1), jnp.float32)
        for h in range(heads):
            cols = slice(h * HEAD_DIM, (h + 1) * HEAD_DIM)
            piece = residual_ref[d, :, cols].astype(jnp.float32) + back_ref[d * heads + h].astype(
                jnp.float32
            )
            pieces.append(piece)
            squares = squares + jnp.sum(piece * piece, axis=1, keepdims=True)
        inv_rms = lax.rsqrt(squares / (heads * HEAD_DIM) + epsilon)
        for h in range(heads):
            cols = slice(h * HEAD_DIM, (h + 1) * HEAD_DIM)
            out_ref[d * tokens : (d + 1) * tokens, cols] = (
                pieces[h] * inv_rms * gain_ref[:, cols]
            ).astype(out_ref.dtype)


def normalized(back, residual, gain):
    docs, tokens, width = residual.shape
    return pl.pallas_call(
        lambda *refs: norm_kernel(docs, width // HEAD_DIM, *refs),
        out_shape=jax.ShapeDtypeStruct((docs * tokens, width), jnp.bfloat16),
        cost_estimate=pl.CostEstimate(
            flops=8 * docs * tokens * width, bytes_accessed=6 * docs * tokens * width, transcendentals=0
        ),
        compiler_params=pltpu.CompilerParams(vmem_limit_bytes=16 << 20),
        name="normalized",
    )(back, residual, gain.reshape(1, width))


def add(*terms):
    return sum(t.astype(jnp.float32) for t in terms).astype(jnp.bfloat16)


def local(
    queries, key_vectors, value_vectors, residual, norm_gain, head_weight, head_bias, doc_lengths
):
    tokens, docs, width = queries.shape
    heads = width // HEAD_DIM
    sizes = [lax.axis_size(axis) for axis in AXES]
    y_size, c_size, _, _, _ = sizes
    _, c_at, _, _, _ = [lax.axis_index(axis) for axis in AXES]

    def by_head(array):
        return jnp.transpose(array.reshape(tokens, docs, heads, HEAD_DIM), (1, 2, 0, 3)).reshape(
            docs * heads, tokens, HEAD_DIM
        )

    def move(array, **by):
        return lax.ppermute(array, AXES, shift_perm(sizes, **by))

    stacked = jnp.stack([by_head(a) for a in (queries, key_vectors, value_vectors)], axis=1)
    qkv = lax.all_to_all(stacked, PLANE, split_axis=0, concat_axis=0, tiled=True)
    key_own, value_own = qkv[:, 1], qkv[:, 2]
    key_left = move(key_own, y=1)
    value_right = move(value_own, y=-1)
    value_left = move(value_own, y=1)
    key_right = move(key_own, y=-1)
    key_far = move(key_left, y=1)
    value_far = move(value_right, y=-1)

    entries = head_weight.shape[1]
    half = entries // 2
    near = move(lax.dynamic_slice_in_dim(head_weight, c_at * half, half, 1), u=1)
    far = move(near, c=1)
    weights = (head_weight, near, far)
    other_bias = move(head_bias.reshape(1, entries), u=1)

    def in_halves(array):
        swapped = jnp.concatenate([array[:, half:], array[:, :half]], axis=1)
        return jnp.where(c_at == 0, array, swapped)

    bias = jnp.concatenate([head_bias.reshape(1, entries), in_halves(other_bias)], axis=1)

    carry = attend_chunks(doc_lengths, qkv, [(qkv, 1), (qkv, 2)], [0], None, False)
    carry = attend_chunks(
        doc_lengths,
        qkv,
        [(key_left, 0), (value_left, 0), (key_right, 0), (value_right, 0)],
        [-1, 1],
        carry,
        False,
    )
    attended = attend_chunks(
        doc_lengths, qkv, [(key_far, 0), (value_far, 0)], [2], carry, True
    )
    back = lax.all_to_all(attended, PLANE, split_axis=0, concat_axis=0, tiled=True)
    inward = jnp.transpose(residual, (1, 0, 2))
    hidden = normalized(back, inward, norm_gain)

    rows = {(0, 0): hidden}
    rows[1, 0] = move(hidden, w=1)
    rows[0, -1] = move(hidden, z=1)
    rows[0, 1] = move(hidden, z=-1)
    rows[1, -1] = move(rows[0, -1], w=1)
    rows[0, 2] = move(rows[0, -1], z=1)
    rows[1, 1] = move(rows[1, 0], z=-1)
    far_first = move(rows[1, -1][:tokens], z=1)
    far_second = move(rows[1, 1][tokens:], z=-1)

    waves = [[(0, 0)], [(1, 0), (0, -1), (0, 1)], [(1, -1), (0, 2), (1, 1)], [(1, 2)]]
    slopes, sums = [], 0.0
    for wave in waves:
        blocks = [far_first, far_second] if wave == [(1, 2)] else [rows[at] for at in wave]
        slope, part = boost(doc_lengths, weights, bias, blocks, wave)
        slopes.append(slope)
        sums = sums + part

    own_sums, other_sums = sums[:, :entries], in_halves(sums[:, entries:])
    ordered = jnp.concatenate([own_sums, other_sums], axis=0)
    swapped = move(jnp.concatenate([other_sums, own_sums], axis=0), u=1)
    ordered = ordered + swapped
    peers = y_size * c_size
    spread = jnp.broadcast_to(ordered[None], (peers,) + ordered.shape)
    gathered = lax.all_to_all(spread, ("y", "c"), split_axis=0, concat_axis=0, tiled=True)
    totals = jnp.sum(gathered, axis=0).reshape(2, docs, entries)
    pooled = jnp.log(totals / doc_lengths[None, :, None].astype(jnp.float32)) / sharpness
    coefficient = 2.0 * flops_weight / docs * jnp.mean(pooled, axis=1)[:, None, :] / totals
    own_pooled = pooled[0]
    coef = jnp.concatenate([coefficient[0], in_halves(coefficient[1])], axis=1)

    block = docs * tokens

    def terms(number, split):
        return gradient(slopes[number], coef, weights, split)

    first, second = terms(3, [tokens, tokens])
    first = move(first, z=-1)
    second = move(second, z=1)
    left, across, right = terms(2, [block] * 3)
    across = move(across, z=-1)
    left = jnp.concatenate([add(left[:tokens], first), left[tokens:]])
    right = jnp.concatenate([right[:tokens], add(right[tokens:], second)])
    left = move(left, w=1)
    right = move(right, z=1)
    pair, before, after = terms(1, [block] * 3)
    after = move(after, z=1)
    pair = move(add(pair, right), w=1)
    before = move(add(before, left, across), z=-1)
    (own,) = terms(0, [block])
    result = add(own, pair, before, after)
    return (own_pooled, jnp.transpose(result.reshape(docs, tokens, width), (1, 0, 2)))


def solution(mesh):
    grid = Mesh(mesh.devices.reshape(4, 2, 2, 2, 4), AXES)
    rows = P(AXES, None, None)
    vocab = ("u", "w", "z")
    in_specs = (rows, rows, rows, rows, P(), P(None, vocab), P(vocab), P())
    out_specs = (P(None, vocab), rows)

    return jax.shard_map(local, mesh=grid, in_specs=in_specs, out_specs=out_specs, check_vma=False)
```

```python
import math

import jax
import jax.numpy as jnp
from jax import lax
from jax.experimental import pallas as pl
from jax.experimental.pallas import tpu as pltpu
from jax.sharding import Mesh
from jax.sharding import PartitionSpec as P


HEAD_DIM = 128
AXES = ("y", "c", "u", "w", "z")
PLANE = ("c", "u", "w", "z")
LOW = -1e30

sharpness = 8.0
flops_weight = 500.0
epsilon = 1e-05


def shift_perm(sizes, **by):
    steps = [by.get(axis, 0) for axis in AXES]
    pairs = []
    for source in range(math.prod(sizes)):
        rest, place = source, []
        for size in reversed(sizes):
            place.append(rest % size)
            rest //= size
        target = 0
        for size, at, step in zip(sizes, reversed(place), steps):
            target = target * size + (at + step) % size
        pairs.append((source, target))
    return pairs


def attention_kernel(first, last, turns, sub, part, lengths, q_ref, *refs):
    chunks = len(turns)
    keys = refs[: 2 * chunks : 2]
    values = refs[1 : 2 * chunks : 2]
    rest = list(refs[2 * chunks :])
    if not first:
        top_in, sum_in = rest.pop(0), rest.pop(0)
    if last:
        out_ref = rest.pop(0)
        top_ref, sum_ref = rest.pop(0), rest.pop(0)
    else:
        top_ref, sum_ref = rest.pop(0), rest.pop(0)
    wide, held = rest.pop(0), rest.pop(0)
    step = pl.program_id(0)
    rows = top_ref.shape[0]
    depth = wide.shape[1]
    scale = math.log2(math.e) / math.sqrt(HEAD_DIM)

    @pl.when(step == 0)
    def _():
        for n in range(chunks):
            wide[n, :, :HEAD_DIM] = values[n][...].reshape(depth, HEAD_DIM)
            wide[n, :, HEAD_DIM:] = jnp.ones((depth, HEAD_DIM), wide.dtype)
            held[n] = keys[n][...].reshape(depth, HEAD_DIM)

    if first:
        top_ref[...] = jnp.full_like(top_ref, LOW)
        sum_ref[...] = jnp.zeros_like(sum_ref)
    else:
        top_ref[...] = top_in[...]
        sum_ref[...] = sum_in[...]
    length = lengths[lax.axis_index("c")]
    y_at, y_size = lax.axis_index("y"), lax.axis_size("y")
    queries_real = length - y_at * depth > step * rows

    def piece(n, at, count, top, summed):
        query = q_ref[pl.ds(at // 64, sub // 64)].reshape(sub, HEAD_DIM)
        for start in range(0, depth, part):
            key = held[n, start : start + part]
            scores = lax.dot_general(
                query, key, (((1,), (1,)), ((), ())), preferred_element_type=jnp.float32
            )
            place = lax.broadcasted_iota(jnp.int32, (1, part), 1) + start
            scores = scores + jnp.where(place < count, 0.0, LOW)
            new_top = jnp.max(scores, axis=1, keepdims=True)
            if top is not None:
                new_top = jnp.maximum(top, new_top)
            weights = jnp.exp2((scores - new_top) * scale)
            added = jnp.dot(
                weights.astype(jnp.bfloat16),
                wide[n, start : start + part],
                preferred_element_type=jnp.float32,
            )
            if top is not None:
                added = summed * jnp.exp2((top - new_top) * scale) + added
            top, summed = new_top, added
        return top, summed

    def before(at):
        return (None, None) if first else (top_ref[pl.ds(at, sub), :1], sum_ref[pl.ds(at, sub), :])

    def after(at, top, summed):
        top_ref[pl.ds(at, sub), :] = jnp.broadcast_to(top, (sub, HEAD_DIM))
        sum_ref[pl.ds(at, sub), :] = summed

    def attend(n, count):
        places = range(0, rows, sub)
        running = [before(at) for at in places]
        done = [piece(n, at, count, *run) for at, run in zip(places, running)]
        for at, run in zip(places, done):
            after(at, *run)

    def chunk(n, carry):
        turn = turns[0] + n * (turns[-1] - turns[0])
        count = length - lax.rem(y_at + turn + y_size, y_size) * depth

        @pl.when(jnp.logical_and(queries_real, count > 0))
        def _():
            attend(n, count)

        return carry

    if chunks == 1:
        chunk(0, 0)
    else:
        lax.fori_loop(0, chunks, chunk, 0)

    if last:

        @pl.when(queries_real)
        def _():
            done = sum_ref[:, :HEAD_DIM] / sum_ref[:, HEAD_DIM:]
            out_ref[...] = done.astype(out_ref.dtype).reshape(out_ref.shape)

        @pl.when(jnp.logical_not(queries_real))
        def _():
            out_ref[...] = jnp.zeros_like(out_ref)


def attend_chunks(lengths, qkv, pairs, turns, carry, last, block=1024, sub=256, part=512):
    sources, tokens = qkv.shape[0], qkv.shape[2]
    total = sources * tokens
    first = carry is None
    chunks = len(pairs) // 2

    def whole(array, which):
        if array.ndim == 4:
            return pl.BlockSpec(
                (sources, None, tokens, HEAD_DIM), lambda i, counts: (0, which, 0, 0)
            )
        return pl.BlockSpec((sources, tokens, HEAD_DIM), lambda i, counts: (0, 0, 0))

    in_specs = [
        pl.BlockSpec((block // tokens, None, tokens, HEAD_DIM), lambda i, counts: (i, 0, 0, 0))
    ]
    operands = [qkv]
    for array, which in pairs:
        in_specs.append(whole(array, which))
        operands.append(array)
    top_spec = pl.BlockSpec((block, HEAD_DIM), lambda i, counts: (i, 0))
    sum_spec = pl.BlockSpec((block, 2 * HEAD_DIM), lambda i, counts: (i, 0))
    if not first:
        in_specs += [top_spec, sum_spec]
        operands += list(carry)
    scratch = [
        pltpu.VMEM((chunks, total, 2 * HEAD_DIM), jnp.bfloat16),
        pltpu.VMEM((chunks, total, HEAD_DIM), jnp.bfloat16),
    ]
    if last:
        out_specs = pl.BlockSpec((block // tokens, tokens, HEAD_DIM), lambda i, counts: (i, 0, 0))
        out_shape = jax.ShapeDtypeStruct((sources, tokens, HEAD_DIM), jnp.bfloat16)
        scratch = [
            pltpu.VMEM((block, HEAD_DIM), jnp.float32),
            pltpu.VMEM((block, 2 * HEAD_DIM), jnp.float32),
        ] + scratch
    else:
        out_specs = [top_spec, sum_spec]
        out_shape = [
            jax.ShapeDtypeStruct((total, HEAD_DIM), jnp.float32),
            jax.ShapeDtypeStruct((total, 2 * HEAD_DIM), jnp.float32),
        ]

    def body(*refs):
        attention_kernel(first, last, turns, sub, part, *refs)

    return pl.pallas_call(
        body,
        grid_spec=pltpu.PrefetchScalarGridSpec(
            num_scalar_prefetch=1,
            grid=(total // block,),
            in_specs=in_specs,
            out_specs=out_specs,
            scratch_shapes=scratch,
        ),
        out_shape=out_shape,
        cost_estimate=pl.CostEstimate(
            flops=8 * total * total * HEAD_DIM * chunks,
            bytes_accessed=4 << 20,
            transcendentals=total * total * chunks,
        ),
        compiler_params=pltpu.CompilerParams(vmem_limit_bytes=24 << 20),
        name="attend_last" if last else ("attend_first" if first else "attend_next"),
    )(lengths, *operands)


def logits_kernel(blocks, places, cols, lengths, own_ref, near_ref, far_ref, bias_ref, *refs):
    rows_in = refs[:blocks]
    slope_ref, total_ref, rows_ref = refs[blocks:]
    at = 0
    for ref in rows_in:
        rows_ref[pl.ds(at, ref.shape[0]), :] = ref[...]
        at += ref.shape[0]
    tokens = 64
    y_at, c_at, u_at, w_at, z_at = [lax.axis_index(axis) for axis in AXES]
    _, c_size, u_size, w_size, z_size = [lax.axis_size(axis) for axis in AXES]
    real = []
    for part in range(rows_ref.shape[0] // tokens):
        w_by, z_by = places[part // 2]
        shard = (y_at * c_size + c_at) * u_size + u_at
        shard = shard * w_size + lax.rem(w_at + w_by, w_size)
        shard = shard * z_size + lax.rem(z_at + z_by + z_size, z_size)
        real.append(lengths[part % 2] - shard * tokens)

    first = 0
    for ref in (own_ref, near_ref, far_ref):

        def tile(index, carry, ref=ref, first=first):
            here = pl.ds(pl.multiple_of(index * cols, cols), cols)
            where = pl.ds(pl.multiple_of(first + index * cols, cols), cols)
            logits = jnp.dot(rows_ref[...], ref[:, here], preferred_element_type=jnp.float32)
            logits = logits + bias_ref[:, where]
            sums = [jnp.zeros((1, cols), jnp.float32)] * 2
            for part in range(rows_ref.shape[0] // tokens):
                piece = logits[part * tokens : (part + 1) * tokens]
                base = 1.0 + jnp.maximum(piece, 0.0)
                power2 = base * base
                power4 = power2 * power2
                place = lax.broadcasted_iota(jnp.int32, piece.shape, 0)
                allowed = place < real[part]
                boosted = jnp.where(allowed, power4 * power4, 0.0)
                slope = jnp.where(
                    jnp.logical_and(allowed, piece > 0.0), power4 * (power2 * base), 0.0
                )
                slope_ref[pl.ds(part * tokens, tokens), where] = slope
                sums[part % 2] = sums[part % 2] + jnp.sum(boosted, axis=0, keepdims=True)
            total_ref[0:1, where] = sums[0]
            total_ref[1:2, where] = sums[1]
            return carry

        lax.fori_loop(0, ref.shape[1] // cols, tile, 0)
        first += ref.shape[1]


def simple_call(body, out_shape, operands, scratch=(), grant=4, flops=0, smem=False):
    nbytes = sum(o.size * o.dtype.itemsize for o in operands)
    in_specs = [pl.BlockSpec(memory_space=pltpu.VMEM)] * len(operands)
    if smem:
        in_specs[0] = pl.BlockSpec(memory_space=pltpu.SMEM)
    return pl.pallas_call(
        body,
        in_specs=in_specs,
        out_specs=jax.tree.map(lambda _: pl.BlockSpec(memory_space=pltpu.VMEM), out_shape),
        out_shape=out_shape,
        scratch_shapes=list(scratch),
        cost_estimate=pl.CostEstimate(flops=flops, bytes_accessed=2 * nbytes, transcendentals=0),
        compiler_params=pltpu.CompilerParams(vmem_limit_bytes=grant << 20),
    )(*operands)


def boost(lengths, weights, bias, blocks, places, cols=256):
    width = weights[0].shape[0]
    entries = sum(w.shape[1] for w in weights)
    rows = sum(b.shape[0] for b in blocks)

    def body(*refs):
        logits_kernel(len(blocks), places, cols, *refs)

    return simple_call(
        body,
        [
            jax.ShapeDtypeStruct((rows, entries), jnp.float32),
            jax.ShapeDtypeStruct((2, entries), jnp.float32),
        ],
        [lengths, *weights, bias, *blocks],
        scratch=[pltpu.VMEM((rows, width), jnp.bfloat16)],
        grant=12,
        flops=4 * max(rows, 256) * width * entries,
        smem=True,
    )


def gradient_kernel(outs, cols, slope_ref, coef_ref, own_ref, near_ref, far_ref, *refs):
    out_refs, slopes = refs[:outs], refs[outs]
    tokens = 64
    for part in range(slopes.shape[0] // tokens):
        where = pl.ds(part * tokens, tokens)
        doc = part % 2
        slopes[where, :] = (coef_ref[doc : doc + 1, :] * slope_ref[where, :]).astype(slopes.dtype)

    def tile(index, carry):
        where = pl.ds(pl.multiple_of(index * cols, cols), cols)
        result, at = None, 0
        for ref in (own_ref, near_ref, far_ref):
            term = lax.dot_general(
                slopes[:, at : at + ref.shape[1]],
                ref[where, :],
                (((1,), (1,)), ((), ())),
                preferred_element_type=jnp.float32,
            )
            result = term if result is None else result + term
            at += ref.shape[1]
        at = 0
        for ref in out_refs:
            ref[:, where] = result[at : at + ref.shape[0]].astype(ref.dtype)
            at += ref.shape[0]
        return carry

    lax.fori_loop(0, own_ref.shape[0] // cols, tile, 0)


def gradient(slope, coefficient, weights, split, cols=256):
    rows, entries = slope.shape
    width = weights[0].shape[0]

    def body(*refs):
        gradient_kernel(len(split), cols, *refs)

    return simple_call(
        body,
        [jax.ShapeDtypeStruct((n, width), jnp.bfloat16) for n in split],
        [slope, coefficient, *weights],
        scratch=[pltpu.VMEM((rows, entries), jnp.bfloat16)],
        grant=12,
        flops=4 * max(rows, 256) * width * entries,
    )


def swap_halves(array):
    half = array.shape[1] // 2
    swapped = jnp.concatenate([array[:, half:], array[:, :half]], axis=1)
    return jnp.where(lax.axis_index("c") == 0, array, swapped)


def own_and_other(parts, entries):
    def body(*refs):
        sums = refs[0][...]
        for ref in refs[1 : len(parts)]:
            sums = sums + ref[...]
        own, other = sums[:, :entries], swap_halves(sums[:, entries:])
        out_ref, swapped_ref = refs[len(parts) :]
        out_ref[0:2, :], out_ref[2:4, :] = own, other
        swapped_ref[0:2, :], swapped_ref[2:4, :] = other, own

    shape = jax.ShapeDtypeStruct((4, entries), jnp.float32)
    return simple_call(body, [shape, shape], parts)


def spread_sum(one, two, peers):
    def body(one_ref, two_ref, out_ref):
        total = one_ref[...] + two_ref[...]
        for n in range(peers):
            out_ref[n] = total

    shape = jax.ShapeDtypeStruct((peers,) + one.shape, jnp.float32)
    return simple_call(body, shape, [one, two])


def pool(lengths, gathered):
    peers, _, entries = gathered.shape
    docs = lengths.shape[0]

    def body(lengths_ref, gathered_ref, pooled_ref, coef_ref):
        totals = gathered_ref[0]
        for n in range(1, peers):
            totals = totals + gathered_ref[n]
        doc = lax.broadcasted_iota(jnp.int32, (docs, 1), 0)
        real = jnp.where(doc == 0, lengths_ref[0], lengths_ref[1]).astype(jnp.float32)
        parts = []
        for n in range(2):
            total = totals[n * docs : (n + 1) * docs]
            pooled = jnp.log(total / real) / sharpness
            if n == 0:
                pooled_ref[...] = pooled
            usage = (pooled[0:1] + pooled[1:2]) / docs
            parts.append(2.0 * flops_weight / docs * usage / total)
        coef_ref[:, :entries] = parts[0]
        coef_ref[:, entries:] = swap_halves(parts[1])

    return simple_call(
        body,
        [
            jax.ShapeDtypeStruct((docs, entries), jnp.float32),
            jax.ShapeDtypeStruct((docs, 2 * entries), jnp.float32),
        ],
        [lengths, gathered],
        smem=True,
    )


def rows_of(array, start, count):
    def body(in_ref, out_ref):
        out_ref[...] = in_ref[start : start + count, :]

    shape = jax.ShapeDtypeStruct((count, array.shape[1]), array.dtype)
    return simple_call(body, shape, [array])


def add(base, *terms, start=0):
    end = start + terms[0].shape[0]

    def body(base_ref, *refs):
        out_ref = refs[-1]
        if start > 0:
            out_ref[:start, :] = base_ref[:start, :]
        if end < base.shape[0]:
            out_ref[end:, :] = base_ref[end:, :]
        total = base_ref[start:end, :].astype(jnp.float32)
        for ref in refs[:-1]:
            total = total + ref[...].astype(jnp.float32)
        out_ref[start:end, :] = total.astype(out_ref.dtype)

    shape = jax.ShapeDtypeStruct(base.shape, base.dtype)
    return simple_call(body, shape, [base, *terms])


def norm_kernel(docs, heads, back_ref, residual_ref, gain_ref, out_ref):
    tokens = residual_ref.shape[1]
    for d in range(docs):
        pieces = []
        squares = jnp.zeros((tokens, 1), jnp.float32)
        for h in range(heads):
            cols = slice(h * HEAD_DIM, (h + 1) * HEAD_DIM)
            piece = residual_ref[d, :, cols].astype(jnp.float32) + back_ref[d * heads + h].astype(
                jnp.float32
            )
            pieces.append(piece)
            squares = squares + jnp.sum(piece * piece, axis=1, keepdims=True)
        inv_rms = lax.rsqrt(squares / (heads * HEAD_DIM) + epsilon)
        for h in range(heads):
            cols = slice(h * HEAD_DIM, (h + 1) * HEAD_DIM)
            out_ref[d * tokens : (d + 1) * tokens, cols] = (
                pieces[h] * inv_rms * gain_ref[:, cols]
            ).astype(out_ref.dtype)


def normalized(back, residual, gain):
    docs, tokens, width = residual.shape
    return pl.pallas_call(
        lambda *refs: norm_kernel(docs, width // HEAD_DIM, *refs),
        out_shape=jax.ShapeDtypeStruct((docs * tokens, width), jnp.bfloat16),
        cost_estimate=pl.CostEstimate(
            flops=8 * docs * tokens * width, bytes_accessed=6 * docs * tokens * width, transcendentals=0
        ),
        compiler_params=pltpu.CompilerParams(vmem_limit_bytes=16 << 20),
        name="normalized",
    )(back, residual, gain.reshape(1, width))


def local(
    queries, key_vectors, value_vectors, residual, norm_gain, head_weight, head_bias, doc_lengths
):
    tokens, docs, width = queries.shape
    heads = width // HEAD_DIM
    sizes = [lax.axis_size(axis) for axis in AXES]
    y_size, c_size, _, _, _ = sizes
    _, c_at, _, _, _ = [lax.axis_index(axis) for axis in AXES]

    def by_head(array):
        return jnp.transpose(array.reshape(tokens, docs, heads, HEAD_DIM), (1, 2, 0, 3)).reshape(
            docs * heads, tokens, HEAD_DIM
        )

    def move(array, **by):
        return lax.ppermute(array, AXES, shift_perm(sizes, **by))

    stacked = jnp.stack([by_head(a) for a in (queries, key_vectors, value_vectors)], axis=1)
    qkv = lax.all_to_all(stacked, PLANE, split_axis=0, concat_axis=0, tiled=True)
    key_own, value_own = qkv[:, 1], qkv[:, 2]
    key_left = move(key_own, y=1)
    value_right = move(value_own, y=-1)
    value_left = move(value_own, y=1)
    key_right = move(key_own, y=-1)
    key_far = move(key_left, y=1)
    value_far = move(value_right, y=-1)

    entries = head_weight.shape[1]
    half = entries // 2
    near = move(lax.dynamic_slice_in_dim(head_weight, c_at * half, half, 1), u=1)
    far = move(near, c=1)
    weights = (head_weight, near, far)
    other_bias = move(head_bias.reshape(1, entries), u=1)

    bias = jnp.concatenate([head_bias.reshape(1, entries), swap_halves(other_bias)], axis=1)

    carry = attend_chunks(doc_lengths, qkv, [(qkv, 1), (qkv, 2)], [0], None, False)
    carry = attend_chunks(
        doc_lengths,
        qkv,
        [(key_left, 0), (value_left, 0), (key_right, 0), (value_right, 0)],
        [-1, 1],
        carry,
        False,
    )
    attended = attend_chunks(
        doc_lengths, qkv, [(key_far, 0), (value_far, 0)], [2], carry, True
    )
    back = lax.all_to_all(attended, PLANE, split_axis=0, concat_axis=0, tiled=True)
    inward = jnp.transpose(residual, (1, 0, 2))
    hidden = normalized(back, inward, norm_gain)

    rows = {(0, 0): hidden}
    rows[1, 0] = move(hidden, w=1)
    rows[0, -1] = move(hidden, z=1)
    rows[0, 1] = move(hidden, z=-1)
    rows[1, -1] = move(rows[0, -1], w=1)
    rows[0, 2] = move(rows[0, -1], z=1)
    rows[1, 1] = move(rows[1, 0], z=-1)
    far_first = move(rows_of(rows[1, -1], 0, tokens), z=1)
    far_second = move(rows_of(rows[1, 1], tokens, tokens), z=-1)

    waves = [[(0, 0)], [(1, 0), (0, -1), (0, 1)], [(1, -1), (0, 2), (1, 1)], [(1, 2)]]
    slopes, sums = [], []
    for wave in waves:
        blocks = [far_first, far_second] if wave == [(1, 2)] else [rows[at] for at in wave]
        slope, part = boost(doc_lengths, weights, bias, blocks, wave)
        slopes.append(slope)
        sums.append(part)

    mine, swapped = own_and_other(sums, entries)
    spread = spread_sum(mine, move(swapped, u=1), y_size * c_size)
    gathered = lax.all_to_all(spread, ("y", "c"), split_axis=0, concat_axis=0, tiled=True)
    own_pooled, coef = pool(doc_lengths, gathered)

    block = docs * tokens

    def terms(number, split):
        return gradient(slopes[number], coef, weights, split)

    first, second = terms(3, [tokens, tokens])
    first = move(first, z=-1)
    second = move(second, z=1)
    left, across, right = terms(2, [block] * 3)
    across = move(across, z=-1)
    left = add(left, first)
    right = add(right, second, start=tokens)
    left = move(left, w=1)
    right = move(right, z=1)
    pair, before, after = terms(1, [block] * 3)
    after = move(after, z=1)
    pair = move(add(pair, right), w=1)
    before = move(add(before, left, across), z=-1)
    (own,) = terms(0, [block])
    result = add(own, pair, before, after)
    return (own_pooled, jnp.transpose(result.reshape(docs, tokens, width), (1, 0, 2)))


def solution(mesh):
    grid = Mesh(mesh.devices.reshape(4, 2, 2, 2, 4), AXES)
    rows = P(AXES, None, None)
    vocab = ("u", "w", "z")
    in_specs = (rows, rows, rows, rows, P(), P(None, vocab), P(vocab), P())
    out_specs = (P(None, vocab), rows)

    return jax.shard_map(local, mesh=grid, in_specs=in_specs, out_specs=out_specs, check_vma=False)
```

```python
import math

import jax
import jax.numpy as jnp
from jax import lax
from jax.experimental import pallas as pl
from jax.experimental.pallas import tpu as pltpu
from jax.sharding import Mesh
from jax.sharding import PartitionSpec as P


HEAD_DIM = 128
AXES = ("y", "c", "u", "w", "z")
PLANE = ("c", "u", "w", "z")
LOW = -1e30

sharpness = 8.0
flops_weight = 500.0
epsilon = 1e-05


def shift_perm(sizes, **by):
    steps = [by.get(axis, 0) for axis in AXES]
    pairs = []
    for source in range(math.prod(sizes)):
        rest, place = source, []
        for size in reversed(sizes):
            place.append(rest % size)
            rest //= size
        target = 0
        for size, at, step in zip(sizes, reversed(place), steps):
            target = target * size + (at + step) % size
        pairs.append((source, target))
    return pairs


def attention_kernel(first, last, turns, sub, part, lengths, q_ref, *refs):
    chunks = len(turns)
    keys = refs[: 2 * chunks : 2]
    values = refs[1 : 2 * chunks : 2]
    rest = list(refs[2 * chunks :])
    if not first:
        top_in, sum_in = rest.pop(0), rest.pop(0)
    if last:
        out_ref = rest.pop(0)
        top_ref, sum_ref = rest.pop(0), rest.pop(0)
    else:
        top_ref, sum_ref = rest.pop(0), rest.pop(0)
    wide, held = rest.pop(0), rest.pop(0)
    step = pl.program_id(0)
    rows = top_ref.shape[0]
    depth = wide.shape[1]
    scale = math.log2(math.e) / math.sqrt(HEAD_DIM)

    @pl.when(step == 0)
    def _():
        for n in range(chunks):
            wide[n, :, :HEAD_DIM] = values[n][...].reshape(depth, HEAD_DIM)
            wide[n, :, HEAD_DIM:] = jnp.ones((depth, HEAD_DIM), wide.dtype)
            held[n] = keys[n][...].reshape(depth, HEAD_DIM)

    if first:
        top_ref[...] = jnp.full_like(top_ref, LOW)
        sum_ref[...] = jnp.zeros_like(sum_ref)
    else:
        top_ref[...] = top_in[...]
        sum_ref[...] = sum_in[...]
    length = lengths[lax.axis_index("c")]
    y_at, y_size = lax.axis_index("y"), lax.axis_size("y")
    queries_real = length - y_at * depth > step * rows

    def piece(n, at, count, top, summed):
        query = q_ref[pl.ds(at // 64, sub // 64)].reshape(sub, HEAD_DIM)
        for start in range(0, depth, part):
            key = held[n, start : start + part]
            scores = lax.dot_general(
                query, key, (((1,), (1,)), ((), ())), preferred_element_type=jnp.float32
            )
            place = lax.broadcasted_iota(jnp.int32, (1, part), 1) + start
            scores = scores + jnp.where(place < count, 0.0, LOW)
            new_top = jnp.max(scores, axis=1, keepdims=True)
            if top is not None:
                new_top = jnp.maximum(top, new_top)
            weights = jnp.exp2((scores - new_top) * scale)
            added = jnp.dot(
                weights.astype(jnp.bfloat16),
                wide[n, start : start + part],
                preferred_element_type=jnp.float32,
            )
            if top is not None:
                added = summed * jnp.exp2((top - new_top) * scale) + added
            top, summed = new_top, added
        return top, summed

    def before(at):
        return (None, None) if first else (top_ref[pl.ds(at, sub), :1], sum_ref[pl.ds(at, sub), :])

    def after(at, top, summed):
        top_ref[pl.ds(at, sub), :] = jnp.broadcast_to(top, (sub, HEAD_DIM))
        sum_ref[pl.ds(at, sub), :] = summed

    def attend(n, count):
        places = range(0, rows, sub)
        running = [before(at) for at in places]
        done = [piece(n, at, count, *run) for at, run in zip(places, running)]
        for at, run in zip(places, done):
            after(at, *run)

    def chunk(n, carry):
        turn = turns[0] + n * (turns[-1] - turns[0])
        count = length - lax.rem(y_at + turn + y_size, y_size) * depth

        @pl.when(jnp.logical_and(queries_real, count > 0))
        def _():
            attend(n, count)

        return carry

    if chunks == 1:
        chunk(0, 0)
    else:
        lax.fori_loop(0, chunks, chunk, 0)

    if last:

        @pl.when(queries_real)
        def _():
            done = sum_ref[:, :HEAD_DIM] / sum_ref[:, HEAD_DIM:]
            out_ref[...] = done.astype(out_ref.dtype).reshape(out_ref.shape)

        @pl.when(jnp.logical_not(queries_real))
        def _():
            out_ref[...] = jnp.zeros_like(out_ref)


def attend_chunks(lengths, qkv, pairs, turns, carry, last, block=1024, sub=256, part=512):
    sources, tokens = qkv.shape[0], qkv.shape[2]
    total = sources * tokens
    first = carry is None
    chunks = len(pairs) // 2

    def whole(array, which):
        if array.ndim == 4:
            return pl.BlockSpec(
                (sources, None, tokens, HEAD_DIM), lambda i, counts: (0, which, 0, 0)
            )
        return pl.BlockSpec((sources, tokens, HEAD_DIM), lambda i, counts: (0, 0, 0))

    in_specs = [
        pl.BlockSpec((block // tokens, None, tokens, HEAD_DIM), lambda i, counts: (i, 0, 0, 0))
    ]
    operands = [qkv]
    for array, which in pairs:
        in_specs.append(whole(array, which))
        operands.append(array)
    top_spec = pl.BlockSpec((block, HEAD_DIM), lambda i, counts: (i, 0))
    sum_spec = pl.BlockSpec((block, 2 * HEAD_DIM), lambda i, counts: (i, 0))
    if not first:
        in_specs += [top_spec, sum_spec]
        operands += list(carry)
    scratch = [
        pltpu.VMEM((chunks, total, 2 * HEAD_DIM), jnp.bfloat16),
        pltpu.VMEM((chunks, total, HEAD_DIM), jnp.bfloat16),
    ]
    if last:
        out_specs = pl.BlockSpec((block // tokens, tokens, HEAD_DIM), lambda i, counts: (i, 0, 0))
        out_shape = jax.ShapeDtypeStruct((sources, tokens, HEAD_DIM), jnp.bfloat16)
        scratch = [
            pltpu.VMEM((block, HEAD_DIM), jnp.float32),
            pltpu.VMEM((block, 2 * HEAD_DIM), jnp.float32),
        ] + scratch
    else:
        out_specs = [top_spec, sum_spec]
        out_shape = [
            jax.ShapeDtypeStruct((total, HEAD_DIM), jnp.float32),
            jax.ShapeDtypeStruct((total, 2 * HEAD_DIM), jnp.float32),
        ]

    def body(*refs):
        attention_kernel(first, last, turns, sub, part, *refs)

    return pl.pallas_call(
        body,
        grid_spec=pltpu.PrefetchScalarGridSpec(
            num_scalar_prefetch=1,
            grid=(total // block,),
            in_specs=in_specs,
            out_specs=out_specs,
            scratch_shapes=scratch,
        ),
        out_shape=out_shape,
        cost_estimate=pl.CostEstimate(
            flops=8 * total * total * HEAD_DIM * chunks,
            bytes_accessed=4 << 20,
            transcendentals=total * total * chunks,
        ),
        compiler_params=pltpu.CompilerParams(vmem_limit_bytes=24 << 20),
        name="attend_last" if last else ("attend_first" if first else "attend_next"),
    )(lengths, *operands)


def logits_kernel(blocks, places, cols, lengths, weights_ref, bias_ref, *refs):
    rows_in = refs[:blocks]
    slope_ref, total_ref, rows_ref = refs[blocks:]
    at = 0
    for ref in rows_in:
        rows_ref[pl.ds(at, ref.shape[0]), :] = ref[...]
        at += ref.shape[0]
    tokens = 64
    y_at, c_at, u_at, w_at, z_at = [lax.axis_index(axis) for axis in AXES]
    _, c_size, u_size, w_size, z_size = [lax.axis_size(axis) for axis in AXES]
    real = []
    for part in range(rows_ref.shape[0] // tokens):
        w_by, z_by = places[part // 2]
        shard = (y_at * c_size + c_at) * u_size + u_at
        shard = shard * w_size + lax.rem(w_at + w_by, w_size)
        shard = shard * z_size + lax.rem(z_at + z_by + z_size, z_size)
        real.append(lengths[part % 2] - shard * tokens)

    def tile(index, carry):
        where = pl.ds(pl.multiple_of(index * cols, cols), cols)
        logits = jnp.dot(rows_ref[...], weights_ref[:, where], preferred_element_type=jnp.float32)
        logits = logits + bias_ref[:, where]
        sums = [jnp.zeros((1, cols), jnp.float32)] * 2
        for part in range(rows_ref.shape[0] // tokens):
            piece = logits[part * tokens : (part + 1) * tokens]
            base = 1.0 + jnp.maximum(piece, 0.0)
            power2 = base * base
            power4 = power2 * power2
            place = lax.broadcasted_iota(jnp.int32, piece.shape, 0)
            allowed = place < real[part]
            boosted = jnp.where(allowed, power4 * power4, 0.0)
            slope = jnp.where(
                jnp.logical_and(allowed, piece > 0.0), power4 * (power2 * base), 0.0
            )
            slope_ref[pl.ds(part * tokens, tokens), where] = slope
            sums[part % 2] = sums[part % 2] + jnp.sum(boosted, axis=0, keepdims=True)
        total_ref[0:1, where] = sums[0]
        total_ref[1:2, where] = sums[1]
        return carry

    lax.fori_loop(0, weights_ref.shape[1] // cols, tile, 0)


def side_by_side(own, near, far, own_bias, other_bias):
    depth, entries = own.shape
    half = near.shape[1]

    def body(own_hbm, near_hbm, far_hbm, own_bias_ref, other_bias_ref, out_ref, bias_ref, sems):
        copies = []
        for n, (source, at) in enumerate(
            ((own_hbm, 0), (near_hbm, entries), (far_hbm, entries + half))
        ):
            copies.append(
                pltpu.make_async_copy(
                    source, out_ref.at[:, at : at + source.shape[1]], sems.at[n]
                )
            )
        for copy in copies:
            copy.start()
        bias_ref[:, :entries] = own_bias_ref[...]
        bias_ref[:, entries:] = swap_halves(other_bias_ref[...])
        for copy in copies:
            copy.wait()

    return pl.pallas_call(
        body,
        in_specs=[pl.BlockSpec(memory_space=pl.ANY)] * 3
        + [pl.BlockSpec(memory_space=pltpu.VMEM)] * 2,
        out_specs=[pl.BlockSpec(memory_space=pltpu.VMEM)] * 2,
        out_shape=[
            jax.ShapeDtypeStruct((depth, 2 * entries), own.dtype),
            jax.ShapeDtypeStruct((1, 2 * entries), jnp.float32),
        ],
        scratch_shapes=[pltpu.SemaphoreType.DMA((3,))],
        cost_estimate=pl.CostEstimate(
            flops=0, bytes_accessed=8 * depth * entries, transcendentals=0
        ),
        compiler_params=pltpu.CompilerParams(vmem_limit_bytes=4 << 20),
        name="side_by_side",
    )(pltpu.with_memory_space_constraint(own, pltpu.HBM), near, far, own_bias, other_bias)


def simple_call(body, out_shape, operands, scratch=(), grant=4, flops=0, smem=False):
    nbytes = sum(o.size * o.dtype.itemsize for o in operands)
    in_specs = [pl.BlockSpec(memory_space=pltpu.VMEM)] * len(operands)
    if smem:
        in_specs[0] = pl.BlockSpec(memory_space=pltpu.SMEM)
    return pl.pallas_call(
        body,
        in_specs=in_specs,
        out_specs=jax.tree.map(lambda _: pl.BlockSpec(memory_space=pltpu.VMEM), out_shape),
        out_shape=out_shape,
        scratch_shapes=list(scratch),
        cost_estimate=pl.CostEstimate(flops=flops, bytes_accessed=2 * nbytes, transcendentals=0),
        compiler_params=pltpu.CompilerParams(vmem_limit_bytes=grant << 20),
    )(*operands)


def boost(lengths, weights, bias, blocks, places, cols=512):
    width, entries = weights.shape
    rows = sum(b.shape[0] for b in blocks)

    def body(*refs):
        logits_kernel(len(blocks), places, cols, *refs)

    return simple_call(
        body,
        [
            jax.ShapeDtypeStruct((rows, entries), jnp.float32),
            jax.ShapeDtypeStruct((2, entries), jnp.float32),
        ],
        [lengths, weights, bias, *blocks],
        scratch=[pltpu.VMEM((rows, width), jnp.bfloat16)],
        grant=12,
        flops=4 * max(rows, 256) * width * entries,
        smem=True,
    )


def gradient_kernel(outs, cols, slope_ref, coef_ref, weights_ref, *refs):
    out_refs, slopes = refs[:outs], refs[outs]
    tokens = 64
    for part in range(slopes.shape[0] // tokens):
        where = pl.ds(part * tokens, tokens)
        doc = part % 2
        slopes[where, :] = (coef_ref[doc : doc + 1, :] * slope_ref[where, :]).astype(slopes.dtype)

    def tile(index, carry):
        where = pl.ds(pl.multiple_of(index * cols, cols), cols)
        result = lax.dot_general(
            slopes[...],
            weights_ref[where, :],
            (((1,), (1,)), ((), ())),
            preferred_element_type=jnp.float32,
        )
        at = 0
        for ref in out_refs:
            ref[:, where] = result[at : at + ref.shape[0]].astype(ref.dtype)
            at += ref.shape[0]
        return carry

    lax.fori_loop(0, weights_ref.shape[0] // cols, tile, 0)


def gradient(slope, coefficient, weights, split, cols=512):
    rows, entries = slope.shape
    width = weights.shape[0]

    def body(*refs):
        gradient_kernel(len(split), cols, *refs)

    return simple_call(
        body,
        [jax.ShapeDtypeStruct((n, width), jnp.bfloat16) for n in split],
        [slope, coefficient, weights],
        scratch=[pltpu.VMEM((rows, entries), jnp.bfloat16)],
        grant=12,
        flops=4 * max(rows, 256) * width * entries,
    )


def swap_halves(array):
    half = array.shape[1] // 2
    swapped = jnp.concatenate([array[:, half:], array[:, :half]], axis=1)
    return jnp.where(lax.axis_index("c") == 0, array, swapped)


def own_and_other(parts, entries):
    def body(*refs):
        sums = refs[0][...]
        for ref in refs[1 : len(parts)]:
            sums = sums + ref[...]
        own, other = sums[:, :entries], swap_halves(sums[:, entries:])
        out_ref, swapped_ref = refs[len(parts) :]
        out_ref[0:2, :], out_ref[2:4, :] = own, other
        swapped_ref[0:2, :], swapped_ref[2:4, :] = other, own

    shape = jax.ShapeDtypeStruct((4, entries), jnp.float32)
    return simple_call(body, [shape, shape], parts)


def spread_sum(one, two, peers):
    def body(one_ref, two_ref, out_ref):
        total = one_ref[...] + two_ref[...]
        for n in range(peers):
            out_ref[n] = total

    shape = jax.ShapeDtypeStruct((peers,) + one.shape, jnp.float32)
    return simple_call(body, shape, [one, two])


def pool(lengths, gathered):
    peers, _, entries = gathered.shape
    docs = lengths.shape[0]

    def body(lengths_ref, gathered_ref, pooled_ref, coef_ref):
        totals = gathered_ref[0]
        for n in range(1, peers):
            totals = totals + gathered_ref[n]
        doc = lax.broadcasted_iota(jnp.int32, (docs, 1), 0)
        real = jnp.where(doc == 0, lengths_ref[0], lengths_ref[1]).astype(jnp.float32)
        parts = []
        for n in range(2):
            total = totals[n * docs : (n + 1) * docs]
            pooled = jnp.log(total / real) / sharpness
            if n == 0:
                pooled_ref[...] = pooled
            usage = (pooled[0:1] + pooled[1:2]) / docs
            parts.append(2.0 * flops_weight / docs * usage / total)
        coef_ref[:, :entries] = parts[0]
        coef_ref[:, entries:] = swap_halves(parts[1])

    return simple_call(
        body,
        [
            jax.ShapeDtypeStruct((docs, entries), jnp.float32),
            jax.ShapeDtypeStruct((docs, 2 * entries), jnp.float32),
        ],
        [lengths, gathered],
        smem=True,
    )


def rows_of(array, start, count):
    def body(in_ref, out_ref):
        out_ref[...] = in_ref[start : start + count, :]

    shape = jax.ShapeDtypeStruct((count, array.shape[1]), array.dtype)
    return simple_call(body, shape, [array])


def add(base, *terms, start=0):
    end = start + terms[0].shape[0]

    def body(base_ref, *refs):
        out_ref = refs[-1]
        if start > 0:
            out_ref[:start, :] = base_ref[:start, :]
        if end < base.shape[0]:
            out_ref[end:, :] = base_ref[end:, :]
        total = base_ref[start:end, :].astype(jnp.float32)
        for ref in refs[:-1]:
            total = total + ref[...].astype(jnp.float32)
        out_ref[start:end, :] = total.astype(out_ref.dtype)

    shape = jax.ShapeDtypeStruct(base.shape, base.dtype)
    return simple_call(body, shape, [base, *terms])


def norm_kernel(docs, heads, back_ref, residual_ref, gain_ref, out_ref):
    tokens = residual_ref.shape[1]
    for d in range(docs):
        pieces = []
        squares = jnp.zeros((tokens, 1), jnp.float32)
        for h in range(heads):
            cols = slice(h * HEAD_DIM, (h + 1) * HEAD_DIM)
            piece = residual_ref[d, :, cols].astype(jnp.float32) + back_ref[d * heads + h].astype(
                jnp.float32
            )
            pieces.append(piece)
            squares = squares + jnp.sum(piece * piece, axis=1, keepdims=True)
        inv_rms = lax.rsqrt(squares / (heads * HEAD_DIM) + epsilon)
        for h in range(heads):
            cols = slice(h * HEAD_DIM, (h + 1) * HEAD_DIM)
            out_ref[d * tokens : (d + 1) * tokens, cols] = (
                pieces[h] * inv_rms * gain_ref[:, cols]
            ).astype(out_ref.dtype)


def normalized(back, residual, gain):
    docs, tokens, width = residual.shape
    return pl.pallas_call(
        lambda *refs: norm_kernel(docs, width // HEAD_DIM, *refs),
        out_shape=jax.ShapeDtypeStruct((docs * tokens, width), jnp.bfloat16),
        cost_estimate=pl.CostEstimate(
            flops=8 * docs * tokens * width, bytes_accessed=6 * docs * tokens * width, transcendentals=0
        ),
        compiler_params=pltpu.CompilerParams(vmem_limit_bytes=16 << 20),
        name="normalized",
    )(back, residual, gain.reshape(1, width))


def local(
    queries, key_vectors, value_vectors, residual, norm_gain, head_weight, head_bias, doc_lengths
):
    tokens, docs, width = queries.shape
    heads = width // HEAD_DIM
    sizes = [lax.axis_size(axis) for axis in AXES]
    y_size, c_size, _, _, _ = sizes
    _, c_at, _, _, _ = [lax.axis_index(axis) for axis in AXES]

    def by_head(array):
        return jnp.transpose(array.reshape(tokens, docs, heads, HEAD_DIM), (1, 2, 0, 3)).reshape(
            docs * heads, tokens, HEAD_DIM
        )

    def move(array, **by):
        return lax.ppermute(array, AXES, shift_perm(sizes, **by))

    stacked = jnp.stack([by_head(a) for a in (queries, key_vectors, value_vectors)], axis=1)
    qkv = lax.all_to_all(stacked, PLANE, split_axis=0, concat_axis=0, tiled=True)
    key_own, value_own = qkv[:, 1], qkv[:, 2]
    key_left = move(key_own, y=1)
    value_right = move(value_own, y=-1)
    value_left = move(value_own, y=1)
    key_right = move(key_own, y=-1)
    key_far = move(key_left, y=1)
    value_far = move(value_right, y=-1)

    entries = head_weight.shape[1]
    half = entries // 2
    near = move(lax.dynamic_slice_in_dim(head_weight, c_at * half, half, 1), u=1)
    far = move(near, c=1)
    own_bias = head_bias.reshape(1, entries)
    other_bias = move(own_bias, u=1)

    carry = attend_chunks(doc_lengths, qkv, [(qkv, 1), (qkv, 2)], [0], None, False)
    carry = attend_chunks(
        doc_lengths,
        qkv,
        [(key_left, 0), (value_left, 0), (key_right, 0), (value_right, 0)],
        [-1, 1],
        carry,
        False,
    )
    attended = attend_chunks(
        doc_lengths, qkv, [(key_far, 0), (value_far, 0)], [2], carry, True
    )
    back = lax.all_to_all(attended, PLANE, split_axis=0, concat_axis=0, tiled=True)
    inward = jnp.transpose(residual, (1, 0, 2))
    hidden = normalized(back, inward, norm_gain)

    rows = {(0, 0): hidden}
    rows[1, 0] = move(hidden, w=1)
    rows[0, -1] = move(hidden, z=1)
    rows[0, 1] = move(hidden, z=-1)
    rows[1, -1] = move(rows[0, -1], w=1)
    rows[0, 2] = move(rows[0, -1], z=1)
    rows[1, 1] = move(rows[1, 0], z=-1)
    far_first = move(rows_of(rows[1, -1], 0, tokens), z=1)
    far_second = move(rows_of(rows[1, 1], tokens, tokens), z=-1)

    weights, bias = side_by_side(head_weight, near, far, own_bias, other_bias)
    waves = [[(0, 0)], [(1, 0), (0, -1), (0, 1)], [(1, -1), (0, 2), (1, 1)], [(1, 2)]]
    slopes, sums = [], []
    for wave in waves:
        blocks = [far_first, far_second] if wave == [(1, 2)] else [rows[at] for at in wave]
        slope, part = boost(doc_lengths, weights, bias, blocks, wave)
        slopes.append(slope)
        sums.append(part)

    mine, swapped = own_and_other(sums, entries)
    spread = spread_sum(mine, move(swapped, u=1), y_size * c_size)
    gathered = lax.all_to_all(spread, ("y", "c"), split_axis=0, concat_axis=0, tiled=True)
    own_pooled, coef = pool(doc_lengths, gathered)

    block = docs * tokens

    def terms(number, split):
        return gradient(slopes[number], coef, weights, split)

    first, second = terms(3, [tokens, tokens])
    first = move(first, z=-1)
    second = move(second, z=1)
    left, across, right = terms(2, [block] * 3)
    across = move(across, z=-1)
    left = add(left, first)
    right = add(right, second, start=tokens)
    left = move(left, w=1)
    right = move(right, z=1)
    pair, before, after = terms(1, [block] * 3)
    after = move(after, z=1)
    pair = move(add(pair, right), w=1)
    before = move(add(before, left, across), z=-1)
    (own,) = terms(0, [block])
    result = add(own, pair, before, after)
    return (own_pooled, jnp.transpose(result.reshape(docs, tokens, width), (1, 0, 2)))


def solution(mesh):
    grid = Mesh(mesh.devices.reshape(4, 2, 2, 2, 4), AXES)
    rows = P(AXES, None, None)
    vocab = ("u", "w", "z")
    in_specs = (rows, rows, rows, rows, P(), P(None, vocab), P(vocab), P())
    out_specs = (P(None, vocab), rows)

    return jax.shard_map(local, mesh=grid, in_specs=in_specs, out_specs=out_specs, check_vma=False)
```

```python
import math

import jax
import jax.numpy as jnp
from jax import lax
from jax.experimental import pallas as pl
from jax.experimental.pallas import tpu as pltpu
from jax.sharding import Mesh
from jax.sharding import PartitionSpec as P


HEAD_DIM = 128
AXES = ("y", "c", "u", "w", "z")
PLANE = ("c", "u", "w", "z")
LOW = -1e30

sharpness = 8.0
flops_weight = 500.0
epsilon = 1e-05


def shift_perm(sizes, **by):
    steps = [by.get(axis, 0) for axis in AXES]
    pairs = []
    for source in range(math.prod(sizes)):
        rest, place = source, []
        for size in reversed(sizes):
            place.append(rest % size)
            rest //= size
        target = 0
        for size, at, step in zip(sizes, reversed(place), steps):
            target = target * size + (at + step) % size
        pairs.append((source, target))
    return pairs


def attention_kernel(first, last, turns, sources, rows, sub, part, lengths, *refs):
    chunks = len(turns)
    arrays, refs = refs[: 1 + 2 * chunks], list(refs[1 + 2 * chunks :])
    carried = [] if first else [refs.pop(0), refs.pop(0)]
    results = [refs.pop(0)] if last else [refs.pop(0), refs.pop(0)]
    query_ref, key_ref, value_ref, wide, sems = refs
    top_ref, sum_ref = carried if last else results
    depth = wide.shape[1]
    tokens = query_ref.shape[1]
    scale = math.log2(math.e) / math.sqrt(HEAD_DIM)

    targets = [query_ref]
    for n in range(chunks):
        targets += [key_ref.at[n], value_ref.at[n]]
    copies = []
    for n, (array, which, target) in enumerate(zip(arrays, sources, targets)):
        source = array if which is None else array.at[:, which]
        copies.append(pltpu.make_async_copy(source, target, sems.at[n]))
    for copy in copies:
        copy.start()
    for n in range(chunks):
        wide[n, :, HEAD_DIM:] = jnp.ones((depth, HEAD_DIM), wide.dtype)
    if first:
        top_ref[...] = jnp.full_like(top_ref, LOW)
        sum_ref[...] = jnp.zeros_like(sum_ref)
    elif not last:
        top_ref[...] = carried[0][...]
        sum_ref[...] = carried[1][...]
    for copy in copies:
        copy.wait()
    for n in range(chunks):
        wide[n, :, :HEAD_DIM] = value_ref[n].reshape(depth, HEAD_DIM)

    length = lengths[lax.axis_index("c")]
    y_at, y_size = lax.axis_index("y"), lax.axis_size("y")

    def piece(n, at, count, top, summed):
        query = query_ref[pl.ds(at // tokens, sub // tokens)].reshape(sub, HEAD_DIM)
        for start in range(0, depth, part):
            key = key_ref[n, start // tokens : (start + part) // tokens].reshape(part, HEAD_DIM)
            scores = lax.dot_general(
                query, key, (((1,), (1,)), ((), ())), preferred_element_type=jnp.float32
            )
            place = lax.broadcasted_iota(jnp.int32, (1, part), 1) + start
            scores = scores + jnp.where(place < count, 0.0, LOW)
            new_top = jnp.max(scores, axis=1, keepdims=True)
            if top is not None:
                new_top = jnp.maximum(top, new_top)
            weights = jnp.exp2((scores - new_top) * scale)
            added = jnp.dot(
                weights.astype(jnp.bfloat16),
                wide[n, start : start + part],
                preferred_element_type=jnp.float32,
            )
            if top is not None:
                added = summed * jnp.exp2((top - new_top) * scale) + added
            top, summed = new_top, added
        return top, summed

    def finish(at, summed):
        done = summed[:, :HEAD_DIM] / summed[:, HEAD_DIM:]
        out = done.astype(results[0].dtype).reshape(sub // tokens, tokens, HEAD_DIM)
        results[0][pl.ds(at // tokens, sub // tokens)] = out

    def attend(index, n, count):
        places = [
            pl.multiple_of(index * rows + at, sub) for at in range(0, rows, sub)
        ]
        running = [
            (None, None) if first else (top_ref[pl.ds(at, sub), :1], sum_ref[pl.ds(at, sub), :])
            for at in places
        ]
        done = [piece(n, at, count, *run) for at, run in zip(places, running)]
        for at, (top, summed) in zip(places, done):
            if last:
                finish(at, summed)
            else:
                top_ref[pl.ds(at, sub), :] = jnp.broadcast_to(top, (sub, HEAD_DIM))
                sum_ref[pl.ds(at, sub), :] = summed

    blocks = depth // rows

    def chunk(step, carry):
        n, index = step // blocks, lax.rem(step, blocks)
        turn = turns[0] + n * (turns[-1] - turns[0])
        count = length - lax.rem(y_at + turn + y_size, y_size) * depth
        queries_real = length - y_at * depth > index * rows

        @pl.when(jnp.logical_and(queries_real, count > 0))
        def _():
            attend(index, 0 if chunks == 1 else n, count)

        if last:

            @pl.when(jnp.logical_and(queries_real, count <= 0))
            def _():
                for at in range(0, rows, sub):
                    at = pl.multiple_of(index * rows + at, sub)
                    finish(at, sum_ref[pl.ds(at, sub), :])

            @pl.when(jnp.logical_not(queries_real))
            def _():
                where = pl.ds(index * (rows // tokens), rows // tokens)
                results[0][where] = jnp.zeros((rows // tokens, tokens, HEAD_DIM), jnp.bfloat16)

        return carry

    lax.fori_loop(0, chunks * blocks, chunk, 0)


def attend_chunks(lengths, qkv, pairs, turns, carry, last, rows=1024, sub=256, part=512):
    blocks, _, tokens, _ = qkv.shape
    total = blocks * tokens
    first = carry is None
    chunks = len(turns)
    arrays = [qkv] + [array for array, _ in pairs]
    sources = [0] + [which for _, which in pairs]
    held = [] if first else list(carry)

    def body(*refs):
        attention_kernel(first, last, turns, sources, rows, sub, part, *refs)

    if last:
        out_shape = [jax.ShapeDtypeStruct((blocks, tokens, HEAD_DIM), jnp.bfloat16)]
    else:
        out_shape = [
            jax.ShapeDtypeStruct((total, HEAD_DIM), jnp.float32),
            jax.ShapeDtypeStruct((total, 2 * HEAD_DIM), jnp.float32),
        ]
    return pl.pallas_call(
        body,
        in_specs=[pl.BlockSpec(memory_space=pltpu.SMEM)]
        + [pl.BlockSpec(memory_space=pl.ANY)] * len(arrays)
        + [pl.BlockSpec(memory_space=pltpu.VMEM)] * len(held),
        out_specs=[pl.BlockSpec(memory_space=pltpu.VMEM)] * len(out_shape),
        out_shape=out_shape,
        scratch_shapes=[
            pltpu.VMEM((blocks, tokens, HEAD_DIM), jnp.bfloat16),
            pltpu.VMEM((chunks, blocks, tokens, HEAD_DIM), jnp.bfloat16),
            pltpu.VMEM((chunks, blocks, tokens, HEAD_DIM), jnp.bfloat16),
            pltpu.VMEM((chunks, total, 2 * HEAD_DIM), jnp.bfloat16),
            pltpu.SemaphoreType.DMA((len(arrays),)),
        ],
        cost_estimate=pl.CostEstimate(
            flops=8 * total * total * HEAD_DIM * chunks,
            bytes_accessed=4 << 20,
            transcendentals=total * total * chunks,
        ),
        compiler_params=pltpu.CompilerParams(vmem_limit_bytes=24 << 20),
        name="attend_last" if last else ("attend_first" if first else "attend_next"),
    )(lengths, *arrays, *held)


def logits_kernel(blocks, places, cols, lengths, weights_ref, bias_ref, *refs):
    rows_in = refs[:blocks]
    slope_ref, total_ref, rows_ref = refs[blocks:]
    at = 0
    for ref in rows_in:
        rows_ref[pl.ds(at, ref.shape[0]), :] = ref[...]
        at += ref.shape[0]
    tokens = 64
    y_at, c_at, u_at, w_at, z_at = [lax.axis_index(axis) for axis in AXES]
    _, c_size, u_size, w_size, z_size = [lax.axis_size(axis) for axis in AXES]
    real = []
    for part in range(rows_ref.shape[0] // tokens):
        w_by, z_by = places[part // 2]
        shard = (y_at * c_size + c_at) * u_size + u_at
        shard = shard * w_size + lax.rem(w_at + w_by, w_size)
        shard = shard * z_size + lax.rem(z_at + z_by + z_size, z_size)
        real.append(lengths[part % 2] - shard * tokens)

    def tile(index, carry):
        where = pl.ds(pl.multiple_of(index * cols, cols), cols)
        logits = jnp.dot(rows_ref[...], weights_ref[:, where], preferred_element_type=jnp.float32)
        logits = logits + bias_ref[:, where]
        sums = [jnp.zeros((1, cols), jnp.float32)] * 2
        for part in range(rows_ref.shape[0] // tokens):
            piece = logits[part * tokens : (part + 1) * tokens]
            base = 1.0 + jnp.maximum(piece, 0.0)
            power2 = base * base
            power4 = power2 * power2
            place = lax.broadcasted_iota(jnp.int32, piece.shape, 0)
            allowed = place < real[part]
            boosted = jnp.where(allowed, power4 * power4, 0.0)
            slope = jnp.where(
                jnp.logical_and(allowed, piece > 0.0), power4 * (power2 * base), 0.0
            )
            slope_ref[pl.ds(part * tokens, tokens), where] = slope
            sums[part % 2] = sums[part % 2] + jnp.sum(boosted, axis=0, keepdims=True)
        total_ref[0:1, where] = sums[0]
        total_ref[1:2, where] = sums[1]
        return carry

    lax.fori_loop(0, weights_ref.shape[1] // cols, tile, 0)


def side_by_side(own, near, far, own_bias, other_bias):
    depth, entries = own.shape
    half = near.shape[1]

    def body(own_hbm, near_hbm, far_hbm, own_bias_ref, other_bias_ref, out_ref, bias_ref, sems):
        copies = []
        for n, (source, at) in enumerate(
            ((own_hbm, 0), (near_hbm, entries), (far_hbm, entries + half))
        ):
            copies.append(
                pltpu.make_async_copy(
                    source, out_ref.at[:, at : at + source.shape[1]], sems.at[n]
                )
            )
        for copy in copies:
            copy.start()
        bias_ref[:, :entries] = own_bias_ref[...]
        bias_ref[:, entries:] = swap_halves(other_bias_ref[...])
        for copy in copies:
            copy.wait()

    return pl.pallas_call(
        body,
        in_specs=[pl.BlockSpec(memory_space=pl.ANY)] * 3
        + [pl.BlockSpec(memory_space=pltpu.VMEM)] * 2,
        out_specs=[pl.BlockSpec(memory_space=pltpu.VMEM)] * 2,
        out_shape=[
            jax.ShapeDtypeStruct((depth, 2 * entries), own.dtype),
            jax.ShapeDtypeStruct((1, 2 * entries), jnp.float32),
        ],
        scratch_shapes=[pltpu.SemaphoreType.DMA((3,))],
        cost_estimate=pl.CostEstimate(
            flops=0, bytes_accessed=8 * depth * entries, transcendentals=0
        ),
        compiler_params=pltpu.CompilerParams(vmem_limit_bytes=4 << 20),
        name="side_by_side",
    )(pltpu.with_memory_space_constraint(own, pltpu.HBM), near, far, own_bias, other_bias)


def simple_call(body, out_shape, operands, scratch=(), grant=4, flops=0, smem=False):
    nbytes = sum(o.size * o.dtype.itemsize for o in operands)
    in_specs = [pl.BlockSpec(memory_space=pltpu.VMEM)] * len(operands)
    if smem:
        in_specs[0] = pl.BlockSpec(memory_space=pltpu.SMEM)
    return pl.pallas_call(
        body,
        in_specs=in_specs,
        out_specs=jax.tree.map(lambda _: pl.BlockSpec(memory_space=pltpu.VMEM), out_shape),
        out_shape=out_shape,
        scratch_shapes=list(scratch),
        cost_estimate=pl.CostEstimate(flops=flops, bytes_accessed=2 * nbytes, transcendentals=0),
        compiler_params=pltpu.CompilerParams(vmem_limit_bytes=grant << 20),
    )(*operands)


def boost(lengths, weights, bias, blocks, places, cols=512):
    width, entries = weights.shape
    rows = sum(b.shape[0] for b in blocks)

    def body(*refs):
        logits_kernel(len(blocks), places, cols, *refs)

    return simple_call(
        body,
        [
            jax.ShapeDtypeStruct((rows, entries), jnp.float32),
            jax.ShapeDtypeStruct((2, entries), jnp.float32),
        ],
        [lengths, weights, bias, *blocks],
        scratch=[pltpu.VMEM((rows, width), jnp.bfloat16)],
        grant=12,
        flops=4 * max(rows, 256) * width * entries,
        smem=True,
    )


def gradient_kernel(outs, cols, slope_ref, coef_ref, weights_ref, *refs):
    out_refs, slopes = refs[:outs], refs[outs]
    tokens = 64
    for part in range(slopes.shape[0] // tokens):
        where = pl.ds(part * tokens, tokens)
        doc = part % 2
        slopes[where, :] = (coef_ref[doc : doc + 1, :] * slope_ref[where, :]).astype(slopes.dtype)

    def tile(index, carry):
        where = pl.ds(pl.multiple_of(index * cols, cols), cols)
        result = lax.dot_general(
            slopes[...],
            weights_ref[where, :],
            (((1,), (1,)), ((), ())),
            preferred_element_type=jnp.float32,
        )
        at = 0
        for ref in out_refs:
            ref[:, where] = result[at : at + ref.shape[0]].astype(ref.dtype)
            at += ref.shape[0]
        return carry

    lax.fori_loop(0, weights_ref.shape[0] // cols, tile, 0)


def gradient(slope, coefficient, weights, split, cols=512):
    rows, entries = slope.shape
    width = weights.shape[0]

    def body(*refs):
        gradient_kernel(len(split), cols, *refs)

    return simple_call(
        body,
        [jax.ShapeDtypeStruct((n, width), jnp.bfloat16) for n in split],
        [slope, coefficient, weights],
        scratch=[pltpu.VMEM((rows, entries), jnp.bfloat16)],
        grant=12,
        flops=4 * max(rows, 256) * width * entries,
    )


def swap_halves(array):
    half = array.shape[1] // 2
    swapped = jnp.concatenate([array[:, half:], array[:, :half]], axis=1)
    return jnp.where(lax.axis_index("c") == 0, array, swapped)


def own_and_other(parts, entries):
    def body(*refs):
        sums = refs[0][...]
        for ref in refs[1 : len(parts)]:
            sums = sums + ref[...]
        own, other = sums[:, :entries], swap_halves(sums[:, entries:])
        out_ref, swapped_ref = refs[len(parts) :]
        out_ref[0:2, :], out_ref[2:4, :] = own, other
        swapped_ref[0:2, :], swapped_ref[2:4, :] = other, own

    shape = jax.ShapeDtypeStruct((4, entries), jnp.float32)
    return simple_call(body, [shape, shape], parts)


def spread_sum(one, two, peers):
    def body(one_ref, two_ref, out_ref):
        total = one_ref[...] + two_ref[...]
        for n in range(peers):
            out_ref[n] = total

    shape = jax.ShapeDtypeStruct((peers,) + one.shape, jnp.float32)
    return simple_call(body, shape, [one, two])


def pool(lengths, gathered):
    peers, _, entries = gathered.shape
    docs = lengths.shape[0]

    def body(lengths_ref, gathered_ref, pooled_ref, coef_ref):
        totals = gathered_ref[0]
        for n in range(1, peers):
            totals = totals + gathered_ref[n]
        doc = lax.broadcasted_iota(jnp.int32, (docs, 1), 0)
        real = jnp.where(doc == 0, lengths_ref[0], lengths_ref[1]).astype(jnp.float32)
        parts = []
        for n in range(2):
            total = totals[n * docs : (n + 1) * docs]
            pooled = jnp.log(total / real) / sharpness
            if n == 0:
                pooled_ref[...] = pooled
            usage = (pooled[0:1] + pooled[1:2]) / docs
            parts.append(2.0 * flops_weight / docs * usage / total)
        coef_ref[:, :entries] = parts[0]
        coef_ref[:, entries:] = swap_halves(parts[1])

    return simple_call(
        body,
        [
            jax.ShapeDtypeStruct((docs, entries), jnp.float32),
            jax.ShapeDtypeStruct((docs, 2 * entries), jnp.float32),
        ],
        [lengths, gathered],
        smem=True,
    )


def rows_of(array, start, count):
    def body(in_ref, out_ref):
        out_ref[...] = in_ref[start : start + count, :]

    shape = jax.ShapeDtypeStruct((count, array.shape[1]), array.dtype)
    return simple_call(body, shape, [array])


def add(base, *terms, start=0):
    end = start + terms[0].shape[0]

    def body(base_ref, *refs):
        out_ref = refs[-1]
        if start > 0:
            out_ref[:start, :] = base_ref[:start, :]
        if end < base.shape[0]:
            out_ref[end:, :] = base_ref[end:, :]
        total = base_ref[start:end, :].astype(jnp.float32)
        for ref in refs[:-1]:
            total = total + ref[...].astype(jnp.float32)
        out_ref[start:end, :] = total.astype(out_ref.dtype)

    shape = jax.ShapeDtypeStruct(base.shape, base.dtype)
    return simple_call(body, shape, [base, *terms])


def norm_kernel(docs, heads, back_ref, residual_ref, gain_ref, out_ref):
    tokens = residual_ref.shape[1]
    for d in range(docs):
        pieces = []
        squares = jnp.zeros((tokens, 1), jnp.float32)
        for h in range(heads):
            cols = slice(h * HEAD_DIM, (h + 1) * HEAD_DIM)
            piece = residual_ref[d, :, cols].astype(jnp.float32) + back_ref[d * heads + h].astype(
                jnp.float32
            )
            pieces.append(piece)
            squares = squares + jnp.sum(piece * piece, axis=1, keepdims=True)
        inv_rms = lax.rsqrt(squares / (heads * HEAD_DIM) + epsilon)
        for h in range(heads):
            cols = slice(h * HEAD_DIM, (h + 1) * HEAD_DIM)
            out_ref[d * tokens : (d + 1) * tokens, cols] = (
                pieces[h] * inv_rms * gain_ref[:, cols]
            ).astype(out_ref.dtype)


def normalized(back, residual, gain):
    docs, tokens, width = residual.shape
    return pl.pallas_call(
        lambda *refs: norm_kernel(docs, width // HEAD_DIM, *refs),
        out_shape=jax.ShapeDtypeStruct((docs * tokens, width), jnp.bfloat16),
        cost_estimate=pl.CostEstimate(
            flops=8 * docs * tokens * width, bytes_accessed=6 * docs * tokens * width, transcendentals=0
        ),
        compiler_params=pltpu.CompilerParams(vmem_limit_bytes=16 << 20),
        name="normalized",
    )(back, residual, gain.reshape(1, width))


def local(
    queries, key_vectors, value_vectors, residual, norm_gain, head_weight, head_bias, doc_lengths
):
    tokens, docs, width = queries.shape
    heads = width // HEAD_DIM
    sizes = [lax.axis_size(axis) for axis in AXES]
    y_size, c_size, _, _, _ = sizes
    _, c_at, _, _, _ = [lax.axis_index(axis) for axis in AXES]

    def by_head(array):
        return jnp.transpose(array.reshape(tokens, docs, heads, HEAD_DIM), (1, 2, 0, 3)).reshape(
            docs * heads, tokens, HEAD_DIM
        )

    def move(array, **by):
        return lax.ppermute(array, AXES, shift_perm(sizes, **by))

    stacked = jnp.stack([by_head(a) for a in (queries, key_vectors, value_vectors)], axis=1)
    qkv = lax.all_to_all(stacked, PLANE, split_axis=0, concat_axis=0, tiled=True)
    key_own, value_own = qkv[:, 1], qkv[:, 2]
    key_left = move(key_own, y=1)
    value_right = move(value_own, y=-1)
    value_left = move(value_own, y=1)
    key_right = move(key_own, y=-1)
    key_far = move(key_left, y=1)
    value_far = move(value_right, y=-1)

    entries = head_weight.shape[1]
    half = entries // 2
    near = move(lax.dynamic_slice_in_dim(head_weight, c_at * half, half, 1), u=1)
    far = move(near, c=1)
    own_bias = head_bias.reshape(1, entries)
    other_bias = move(own_bias, u=1)

    carry = attend_chunks(doc_lengths, qkv, [(qkv, 1), (qkv, 2)], [0], None, False)
    carry = attend_chunks(
        doc_lengths,
        qkv,
        [(key_left, None), (value_left, None), (key_right, None), (value_right, None)],
        [-1, 1],
        carry,
        False,
    )
    (attended,) = attend_chunks(
        doc_lengths, qkv, [(key_far, None), (value_far, None)], [2], carry, True
    )
    back = lax.all_to_all(attended, PLANE, split_axis=0, concat_axis=0, tiled=True)
    inward = jnp.transpose(residual, (1, 0, 2))
    hidden = normalized(back, inward, norm_gain)

    rows = {(0, 0): hidden}
    rows[1, 0] = move(hidden, w=1)
    rows[0, -1] = move(hidden, z=1)
    rows[0, 1] = move(hidden, z=-1)
    rows[1, -1] = move(rows[0, -1], w=1)
    rows[0, 2] = move(rows[0, -1], z=1)
    rows[1, 1] = move(rows[1, 0], z=-1)
    far_first = move(rows_of(rows[1, -1], 0, tokens), z=1)
    far_second = move(rows_of(rows[1, 1], tokens, tokens), z=-1)

    weights, bias = side_by_side(head_weight, near, far, own_bias, other_bias)
    waves = [[(0, 0)], [(1, 0), (0, -1), (0, 1)], [(1, -1), (0, 2), (1, 1)], [(1, 2)]]
    slopes, sums = [], []
    for wave in waves:
        blocks = [far_first, far_second] if wave == [(1, 2)] else [rows[at] for at in wave]
        slope, part = boost(doc_lengths, weights, bias, blocks, wave)
        slopes.append(slope)
        sums.append(part)

    mine, swapped = own_and_other(sums, entries)
    spread = spread_sum(mine, move(swapped, u=1), y_size * c_size)
    gathered = lax.all_to_all(spread, ("y", "c"), split_axis=0, concat_axis=0, tiled=True)
    own_pooled, coef = pool(doc_lengths, gathered)

    block = docs * tokens

    def terms(number, split):
        return gradient(slopes[number], coef, weights, split)

    first, second = terms(3, [tokens, tokens])
    first = move(first, z=-1)
    second = move(second, z=1)
    left, across, right = terms(2, [block] * 3)
    across = move(across, z=-1)
    left = add(left, first)
    right = add(right, second, start=tokens)
    left = move(left, w=1)
    right = move(right, z=1)
    pair, before, after = terms(1, [block] * 3)
    after = move(after, z=1)
    pair = move(add(pair, right), w=1)
    before = move(add(before, left, across), z=-1)
    (own,) = terms(0, [block])
    result = add(own, pair, before, after)
    return (own_pooled, jnp.transpose(result.reshape(docs, tokens, width), (1, 0, 2)))


def solution(mesh):
    grid = Mesh(mesh.devices.reshape(4, 2, 2, 2, 4), AXES)
    rows = P(AXES, None, None)
    vocab = ("u", "w", "z")
    in_specs = (rows, rows, rows, rows, P(), P(None, vocab), P(vocab), P())
    out_specs = (P(None, vocab), rows)

    return jax.shard_map(local, mesh=grid, in_specs=in_specs, out_specs=out_specs, check_vma=False)
```

```python
import math

import jax
import jax.numpy as jnp
from jax import lax
from jax.experimental import pallas as pl
from jax.experimental.pallas import tpu as pltpu
from jax.sharding import Mesh
from jax.sharding import PartitionSpec as P


HEAD_DIM = 128
AXES = ("y", "c", "u", "w", "z")
PLANE = ("c", "u", "w", "z")
LOW = -1e30

sharpness = 8.0
flops_weight = 500.0
epsilon = 1e-05


def shift_perm(sizes, **by):
    steps = [by.get(axis, 0) for axis in AXES]
    pairs = []
    for source in range(math.prod(sizes)):
        rest, place = source, []
        for size in reversed(sizes):
            place.append(rest % size)
            rest //= size
        target = 0
        for size, at, step in zip(sizes, reversed(place), steps):
            target = target * size + (at + step) % size
        pairs.append((source, target))
    return pairs


def attention_kernel(first, last, turns, sources, rows, sub, part, lengths, *refs):
    chunks = len(turns)
    arrays, refs = refs[: 1 + 2 * chunks], list(refs[1 + 2 * chunks :])
    carried = [] if first else [refs.pop(0), refs.pop(0)]
    results = [refs.pop(0)] if last else [refs.pop(0), refs.pop(0)]
    query_ref, key_ref, value_ref, wide, sems = refs
    top_ref, sum_ref = carried if last else results
    depth = wide.shape[1]
    tokens = query_ref.shape[1]
    scale = math.log2(math.e) / math.sqrt(HEAD_DIM)

    targets = [query_ref]
    for n in range(chunks):
        targets += [key_ref.at[n], value_ref.at[n]]
    copies = []
    for n, (array, which, target) in enumerate(zip(arrays, sources, targets)):
        source = array if which is None else array.at[:, which]
        copies.append(pltpu.make_async_copy(source, target, sems.at[n]))
    for copy in copies:
        copy.start()
    for n in range(chunks):
        wide[n, :, HEAD_DIM:] = jnp.ones((depth, HEAD_DIM), wide.dtype)
    if first:
        top_ref[...] = jnp.full_like(top_ref, LOW)
        sum_ref[...] = jnp.zeros_like(sum_ref)
    elif not last:
        top_ref[...] = carried[0][...]
        sum_ref[...] = carried[1][...]
    for copy in copies:
        copy.wait()
    for n in range(chunks):
        wide[n, :, :HEAD_DIM] = value_ref[n].reshape(depth, HEAD_DIM)

    length = lengths[lax.axis_index("c")]
    y_at, y_size = lax.axis_index("y"), lax.axis_size("y")

    def piece(n, at, count):
        top, summed = None, None
        query = query_ref[pl.ds(at // tokens, sub // tokens)].reshape(sub, HEAD_DIM)
        for start in range(0, depth, part):
            key = key_ref[n, start // tokens : (start + part) // tokens].reshape(part, HEAD_DIM)
            scores = lax.dot_general(
                query, key, (((1,), (1,)), ((), ())), preferred_element_type=jnp.float32
            )
            place = lax.broadcasted_iota(jnp.int32, (1, part), 1) + start
            scores = scores + jnp.where(place < count, 0.0, LOW)
            new_top = jnp.max(scores, axis=1, keepdims=True)
            if top is not None:
                new_top = jnp.maximum(top, new_top)
            weights = jnp.exp2((scores - new_top) * scale)
            added = jnp.dot(
                weights.astype(jnp.bfloat16),
                wide[n, start : start + part],
                preferred_element_type=jnp.float32,
            )
            if top is not None:
                added = summed * jnp.exp2((top - new_top) * scale) + added
            top, summed = new_top, added
        return top, summed

    def finish(at, summed):
        done = summed[:, :HEAD_DIM] / summed[:, HEAD_DIM:]
        out = done.astype(results[0].dtype).reshape(sub // tokens, tokens, HEAD_DIM)
        results[0][pl.ds(at // tokens, sub // tokens)] = out

    def attend(index, n, count):
        places = [
            pl.multiple_of(index * rows + at, sub) for at in range(0, rows, sub)
        ]
        done = [piece(n, at, count) for at in places]
        for at, (top, summed) in zip(places, done):
            if not first:
                old_top = top_ref[pl.ds(at, sub), :1]
                new_top = jnp.maximum(old_top, top)
                summed = sum_ref[pl.ds(at, sub), :] * jnp.exp2(
                    (old_top - new_top) * scale
                ) + summed * jnp.exp2((top - new_top) * scale)
                top = new_top
            if last:
                finish(at, summed)
            else:
                top_ref[pl.ds(at, sub), :] = jnp.broadcast_to(top, (sub, HEAD_DIM))
                sum_ref[pl.ds(at, sub), :] = summed

    blocks = depth // rows

    def chunk(step, carry):
        n, index = step // blocks, lax.rem(step, blocks)
        turn = turns[0] + n * (turns[-1] - turns[0])
        count = length - lax.rem(y_at + turn + y_size, y_size) * depth
        queries_real = length - y_at * depth > index * rows

        @pl.when(jnp.logical_and(queries_real, count > 0))
        def _():
            attend(index, 0 if chunks == 1 else n, count)

        if last:

            @pl.when(jnp.logical_and(queries_real, count <= 0))
            def _():
                for at in range(0, rows, sub):
                    at = pl.multiple_of(index * rows + at, sub)
                    finish(at, sum_ref[pl.ds(at, sub), :])

            @pl.when(jnp.logical_not(queries_real))
            def _():
                where = pl.ds(index * (rows // tokens), rows // tokens)
                results[0][where] = jnp.zeros((rows // tokens, tokens, HEAD_DIM), jnp.bfloat16)

        return carry

    lax.fori_loop(0, chunks * blocks, chunk, 0)


def attend_chunks(lengths, qkv, pairs, turns, carry, last, rows=1024, sub=256, part=512):
    blocks, _, tokens, _ = qkv.shape
    total = blocks * tokens
    first = carry is None
    chunks = len(turns)
    arrays = [qkv] + [array for array, _ in pairs]
    sources = [0] + [which for _, which in pairs]
    held = [] if first else list(carry)

    def body(*refs):
        attention_kernel(first, last, turns, sources, rows, sub, part, *refs)

    if last:
        out_shape = [jax.ShapeDtypeStruct((blocks, tokens, HEAD_DIM), jnp.bfloat16)]
    else:
        out_shape = [
            jax.ShapeDtypeStruct((total, HEAD_DIM), jnp.float32),
            jax.ShapeDtypeStruct((total, 2 * HEAD_DIM), jnp.float32),
        ]
    return pl.pallas_call(
        body,
        in_specs=[pl.BlockSpec(memory_space=pltpu.SMEM)]
        + [pl.BlockSpec(memory_space=pl.ANY)] * len(arrays)
        + [pl.BlockSpec(memory_space=pltpu.VMEM)] * len(held),
        out_specs=[pl.BlockSpec(memory_space=pltpu.VMEM)] * len(out_shape),
        out_shape=out_shape,
        scratch_shapes=[
            pltpu.VMEM((blocks, tokens, HEAD_DIM), jnp.bfloat16),
            pltpu.VMEM((chunks, blocks, tokens, HEAD_DIM), jnp.bfloat16),
            pltpu.VMEM((chunks, blocks, tokens, HEAD_DIM), jnp.bfloat16),
            pltpu.VMEM((chunks, total, 2 * HEAD_DIM), jnp.bfloat16),
            pltpu.SemaphoreType.DMA((len(arrays),)),
        ],
        cost_estimate=pl.CostEstimate(
            flops=8 * total * total * HEAD_DIM * chunks,
            bytes_accessed=4 << 20,
            transcendentals=total * total * chunks,
        ),
        compiler_params=pltpu.CompilerParams(vmem_limit_bytes=24 << 20),
        name="attend_last" if last else ("attend_first" if first else "attend_next"),
    )(lengths, *arrays, *held)


def logits_kernel(blocks, places, cols, lengths, weights_ref, bias_ref, *refs):
    rows_in = refs[:blocks]
    slope_ref, total_ref, rows_ref = refs[blocks:]
    at = 0
    for ref in rows_in:
        rows_ref[pl.ds(at, ref.shape[0]), :] = ref[...]
        at += ref.shape[0]
    tokens = 64
    y_at, c_at, u_at, w_at, z_at = [lax.axis_index(axis) for axis in AXES]
    _, c_size, u_size, w_size, z_size = [lax.axis_size(axis) for axis in AXES]
    real = []
    for part in range(rows_ref.shape[0] // tokens):
        w_by, z_by = places[part // 2]
        shard = (y_at * c_size + c_at) * u_size + u_at
        shard = shard * w_size + lax.rem(w_at + w_by, w_size)
        shard = shard * z_size + lax.rem(z_at + z_by + z_size, z_size)
        real.append(lengths[part % 2] - shard * tokens)

    def tile(index, carry):
        where = pl.ds(pl.multiple_of(index * cols, cols), cols)
        logits = jnp.dot(rows_ref[...], weights_ref[:, where], preferred_element_type=jnp.float32)
        logits = logits + bias_ref[:, where]
        sums = [jnp.zeros((1, cols), jnp.float32)] * 2
        for part in range(rows_ref.shape[0] // tokens):
            piece = logits[part * tokens : (part + 1) * tokens]
            base = 1.0 + jnp.maximum(piece, 0.0)
            power2 = base * base
            power4 = power2 * power2
            place = lax.broadcasted_iota(jnp.int32, piece.shape, 0)
            allowed = place < real[part]
            boosted = jnp.where(allowed, power4 * power4, 0.0)
            slope = jnp.where(
                jnp.logical_and(allowed, piece > 0.0), power4 * (power2 * base), 0.0
            )
            slope_ref[pl.ds(part * tokens, tokens), where] = slope
            sums[part % 2] = sums[part % 2] + jnp.sum(boosted, axis=0, keepdims=True)
        total_ref[0:1, where] = sums[0]
        total_ref[1:2, where] = sums[1]
        return carry

    lax.fori_loop(0, weights_ref.shape[1] // cols, tile, 0)


def side_by_side(own, near, far, own_bias, other_bias):
    depth, entries = own.shape
    half = near.shape[1]

    def body(own_hbm, near_hbm, far_hbm, own_bias_ref, other_bias_ref, out_ref, bias_ref, sems):
        copies = []
        for n, (source, at) in enumerate(
            ((own_hbm, 0), (near_hbm, entries), (far_hbm, entries + half))
        ):
            copies.append(
                pltpu.make_async_copy(
                    source, out_ref.at[:, at : at + source.shape[1]], sems.at[n]
                )
            )
        for copy in copies:
            copy.start()
        bias_ref[:, :entries] = own_bias_ref[...]
        bias_ref[:, entries:] = swap_halves(other_bias_ref[...])
        for copy in copies:
            copy.wait()

    return pl.pallas_call(
        body,
        in_specs=[pl.BlockSpec(memory_space=pl.ANY)] * 3
        + [pl.BlockSpec(memory_space=pltpu.VMEM)] * 2,
        out_specs=[pl.BlockSpec(memory_space=pltpu.VMEM)] * 2,
        out_shape=[
            jax.ShapeDtypeStruct((depth, 2 * entries), own.dtype),
            jax.ShapeDtypeStruct((1, 2 * entries), jnp.float32),
        ],
        scratch_shapes=[pltpu.SemaphoreType.DMA((3,))],
        cost_estimate=pl.CostEstimate(
            flops=0, bytes_accessed=8 * depth * entries, transcendentals=0
        ),
        compiler_params=pltpu.CompilerParams(vmem_limit_bytes=4 << 20),
        name="side_by_side",
    )(pltpu.with_memory_space_constraint(own, pltpu.HBM), near, far, own_bias, other_bias)


def simple_call(body, out_shape, operands, scratch=(), grant=4, flops=0, smem=False):
    nbytes = sum(o.size * o.dtype.itemsize for o in operands)
    in_specs = [pl.BlockSpec(memory_space=pltpu.VMEM)] * len(operands)
    if smem:
        in_specs[0] = pl.BlockSpec(memory_space=pltpu.SMEM)
    return pl.pallas_call(
        body,
        in_specs=in_specs,
        out_specs=jax.tree.map(lambda _: pl.BlockSpec(memory_space=pltpu.VMEM), out_shape),
        out_shape=out_shape,
        scratch_shapes=list(scratch),
        cost_estimate=pl.CostEstimate(flops=flops, bytes_accessed=2 * nbytes, transcendentals=0),
        compiler_params=pltpu.CompilerParams(vmem_limit_bytes=grant << 20),
    )(*operands)


def boost(lengths, weights, bias, blocks, places, cols=512):
    width, entries = weights.shape
    rows = sum(b.shape[0] for b in blocks)

    def body(*refs):
        logits_kernel(len(blocks), places, cols, *refs)

    return simple_call(
        body,
        [
            jax.ShapeDtypeStruct((rows, entries), jnp.float32),
            jax.ShapeDtypeStruct((2, entries), jnp.float32),
        ],
        [lengths, weights, bias, *blocks],
        scratch=[pltpu.VMEM((rows, width), jnp.bfloat16)],
        grant=12,
        flops=4 * max(rows, 256) * width * entries,
        smem=True,
    )


def gradient_kernel(outs, cols, slope_ref, coef_ref, weights_ref, *refs):
    out_refs, slopes = refs[:outs], refs[outs]
    tokens = 64
    for part in range(slopes.shape[0] // tokens):
        where = pl.ds(part * tokens, tokens)
        doc = part % 2
        slopes[where, :] = (coef_ref[doc : doc + 1, :] * slope_ref[where, :]).astype(slopes.dtype)

    def tile(index, carry):
        where = pl.ds(pl.multiple_of(index * cols, cols), cols)
        result = lax.dot_general(
            slopes[...],
            weights_ref[where, :],
            (((1,), (1,)), ((), ())),
            preferred_element_type=jnp.float32,
        )
        at = 0
        for ref in out_refs:
            ref[:, where] = result[at : at + ref.shape[0]].astype(ref.dtype)
            at += ref.shape[0]
        return carry

    lax.fori_loop(0, weights_ref.shape[0] // cols, tile, 0)


def gradient(slope, coefficient, weights, split, cols=512):
    rows, entries = slope.shape
    width = weights.shape[0]

    def body(*refs):
        gradient_kernel(len(split), cols, *refs)

    return simple_call(
        body,
        [jax.ShapeDtypeStruct((n, width), jnp.bfloat16) for n in split],
        [slope, coefficient, weights],
        scratch=[pltpu.VMEM((rows, entries), jnp.bfloat16)],
        grant=12,
        flops=4 * max(rows, 256) * width * entries,
    )


def swap_halves(array):
    half = array.shape[1] // 2
    swapped = jnp.concatenate([array[:, half:], array[:, :half]], axis=1)
    return jnp.where(lax.axis_index("c") == 0, array, swapped)


def own_and_other(parts, entries):
    def body(*refs):
        sums = refs[0][...]
        for ref in refs[1 : len(parts)]:
            sums = sums + ref[...]
        own, other = sums[:, :entries], swap_halves(sums[:, entries:])
        out_ref, swapped_ref = refs[len(parts) :]
        out_ref[0:2, :], out_ref[2:4, :] = own, other
        swapped_ref[0:2, :], swapped_ref[2:4, :] = other, own

    shape = jax.ShapeDtypeStruct((4, entries), jnp.float32)
    return simple_call(body, [shape, shape], parts)


def spread_sum(one, two, peers):
    def body(one_ref, two_ref, out_ref):
        total = one_ref[...] + two_ref[...]
        for n in range(peers):
            out_ref[n] = total

    shape = jax.ShapeDtypeStruct((peers,) + one.shape, jnp.float32)
    return simple_call(body, shape, [one, two])


def pool(lengths, gathered):
    peers, _, entries = gathered.shape
    docs = lengths.shape[0]

    def body(lengths_ref, gathered_ref, pooled_ref, coef_ref):
        totals = gathered_ref[0]
        for n in range(1, peers):
            totals = totals + gathered_ref[n]
        doc = lax.broadcasted_iota(jnp.int32, (docs, 1), 0)
        real = jnp.where(doc == 0, lengths_ref[0], lengths_ref[1]).astype(jnp.float32)
        parts = []
        for n in range(2):
            total = totals[n * docs : (n + 1) * docs]
            pooled = jnp.log(total / real) / sharpness
            if n == 0:
                pooled_ref[...] = pooled
            usage = (pooled[0:1] + pooled[1:2]) / docs
            parts.append(2.0 * flops_weight / docs * usage / total)
        coef_ref[:, :entries] = parts[0]
        coef_ref[:, entries:] = swap_halves(parts[1])

    return simple_call(
        body,
        [
            jax.ShapeDtypeStruct((docs, entries), jnp.float32),
            jax.ShapeDtypeStruct((docs, 2 * entries), jnp.float32),
        ],
        [lengths, gathered],
        smem=True,
    )


def rows_of(array, start, count):
    def body(in_ref, out_ref):
        out_ref[...] = in_ref[start : start + count, :]

    shape = jax.ShapeDtypeStruct((count, array.shape[1]), array.dtype)
    return simple_call(body, shape, [array])


def add(base, *terms, start=0):
    end = start + terms[0].shape[0]

    def body(base_ref, *refs):
        out_ref = refs[-1]
        if start > 0:
            out_ref[:start, :] = base_ref[:start, :]
        if end < base.shape[0]:
            out_ref[end:, :] = base_ref[end:, :]
        total = base_ref[start:end, :].astype(jnp.float32)
        for ref in refs[:-1]:
            total = total + ref[...].astype(jnp.float32)
        out_ref[start:end, :] = total.astype(out_ref.dtype)

    shape = jax.ShapeDtypeStruct(base.shape, base.dtype)
    return simple_call(body, shape, [base, *terms])


def norm_kernel(docs, heads, back_ref, residual_ref, gain_ref, out_ref):
    tokens = residual_ref.shape[1]
    for d in range(docs):
        pieces = []
        squares = jnp.zeros((tokens, 1), jnp.float32)
        for h in range(heads):
            cols = slice(h * HEAD_DIM, (h + 1) * HEAD_DIM)
            piece = residual_ref[d, :, cols].astype(jnp.float32) + back_ref[d * heads + h].astype(
                jnp.float32
            )
            pieces.append(piece)
            squares = squares + jnp.sum(piece * piece, axis=1, keepdims=True)
        inv_rms = lax.rsqrt(squares / (heads * HEAD_DIM) + epsilon)
        for h in range(heads):
            cols = slice(h * HEAD_DIM, (h + 1) * HEAD_DIM)
            out_ref[d * tokens : (d + 1) * tokens, cols] = (
                pieces[h] * inv_rms * gain_ref[:, cols]
            ).astype(out_ref.dtype)


def normalized(back, residual, gain):
    docs, tokens, width = residual.shape
    return pl.pallas_call(
        lambda *refs: norm_kernel(docs, width // HEAD_DIM, *refs),
        out_shape=jax.ShapeDtypeStruct((docs * tokens, width), jnp.bfloat16),
        cost_estimate=pl.CostEstimate(
            flops=8 * docs * tokens * width, bytes_accessed=6 * docs * tokens * width, transcendentals=0
        ),
        compiler_params=pltpu.CompilerParams(vmem_limit_bytes=16 << 20),
        name="normalized",
    )(back, residual, gain.reshape(1, width))


def local(
    queries, key_vectors, value_vectors, residual, norm_gain, head_weight, head_bias, doc_lengths
):
    tokens, docs, width = queries.shape
    heads = width // HEAD_DIM
    sizes = [lax.axis_size(axis) for axis in AXES]
    y_size, c_size, _, _, _ = sizes
    _, c_at, _, _, _ = [lax.axis_index(axis) for axis in AXES]

    def by_head(array):
        return jnp.transpose(array.reshape(tokens, docs, heads, HEAD_DIM), (1, 2, 0, 3)).reshape(
            docs * heads, tokens, HEAD_DIM
        )

    def move(array, **by):
        return lax.ppermute(array, AXES, shift_perm(sizes, **by))

    stacked = jnp.stack([by_head(a) for a in (queries, key_vectors, value_vectors)], axis=1)
    qkv = lax.all_to_all(stacked, PLANE, split_axis=0, concat_axis=0, tiled=True)
    key_own, value_own = qkv[:, 1], qkv[:, 2]
    key_left = move(key_own, y=1)
    value_right = move(value_own, y=-1)
    value_left = move(value_own, y=1)
    key_right = move(key_own, y=-1)
    key_far = move(key_left, y=1)
    value_far = move(value_right, y=-1)

    entries = head_weight.shape[1]
    half = entries // 2
    near = move(lax.dynamic_slice_in_dim(head_weight, c_at * half, half, 1), u=1)
    far = move(near, c=1)
    own_bias = head_bias.reshape(1, entries)
    other_bias = move(own_bias, u=1)

    carry = attend_chunks(doc_lengths, qkv, [(qkv, 1), (qkv, 2)], [0], None, False)
    carry = attend_chunks(
        doc_lengths,
        qkv,
        [(key_left, None), (value_left, None), (key_right, None), (value_right, None)],
        [-1, 1],
        carry,
        False,
    )
    (attended,) = attend_chunks(
        doc_lengths, qkv, [(key_far, None), (value_far, None)], [2], carry, True
    )
    back = lax.all_to_all(attended, PLANE, split_axis=0, concat_axis=0, tiled=True)
    inward = jnp.transpose(residual, (1, 0, 2))
    hidden = normalized(back, inward, norm_gain)

    rows = {(0, 0): hidden}
    rows[1, 0] = move(hidden, w=1)
    rows[0, -1] = move(hidden, z=1)
    rows[0, 1] = move(hidden, z=-1)
    rows[1, -1] = move(rows[0, -1], w=1)
    rows[0, 2] = move(rows[0, -1], z=1)
    rows[1, 1] = move(rows[1, 0], z=-1)
    far_first = move(rows_of(rows[1, -1], 0, tokens), z=1)
    far_second = move(rows_of(rows[1, 1], tokens, tokens), z=-1)

    weights, bias = side_by_side(head_weight, near, far, own_bias, other_bias)
    waves = [[(0, 0)], [(1, 0), (0, -1), (0, 1)], [(1, -1), (0, 2), (1, 1)], [(1, 2)]]
    slopes, sums = [], []
    for wave in waves:
        blocks = [far_first, far_second] if wave == [(1, 2)] else [rows[at] for at in wave]
        slope, part = boost(doc_lengths, weights, bias, blocks, wave)
        slopes.append(slope)
        sums.append(part)

    mine, swapped = own_and_other(sums, entries)
    spread = spread_sum(mine, move(swapped, u=1), y_size * c_size)
    gathered = lax.all_to_all(spread, ("y", "c"), split_axis=0, concat_axis=0, tiled=True)
    own_pooled, coef = pool(doc_lengths, gathered)

    block = docs * tokens

    def terms(number, split):
        return gradient(slopes[number], coef, weights, split)

    first, second = terms(3, [tokens, tokens])
    first = move(first, z=-1)
    second = move(second, z=1)
    left, across, right = terms(2, [block] * 3)
    across = move(across, z=-1)
    left = add(left, first)
    right = add(right, second, start=tokens)
    left = move(left, w=1)
    right = move(right, z=1)
    pair, before, after = terms(1, [block] * 3)
    after = move(after, z=1)
    pair = move(add(pair, right), w=1)
    before = move(add(before, left, across), z=-1)
    (own,) = terms(0, [block])
    result = add(own, pair, before, after)
    return (own_pooled, jnp.transpose(result.reshape(docs, tokens, width), (1, 0, 2)))


def solution(mesh):
    grid = Mesh(mesh.devices.reshape(4, 2, 2, 2, 4), AXES)
    rows = P(AXES, None, None)
    vocab = ("u", "w", "z")
    in_specs = (rows, rows, rows, rows, P(), P(None, vocab), P(vocab), P())
    out_specs = (P(None, vocab), rows)

    return jax.shard_map(local, mesh=grid, in_specs=in_specs, out_specs=out_specs, check_vma=False)
```
